128 devices in a mesh: space: 32 (over x, y, core), tm: 2 (over z_hi), op: 2 (over z_lo).
Axes of the slice: x: 4, y: 4, z: 4 (z_hi: 2, z_lo: 2; z = z_hi * 2 + z_lo), core: 2. Of those that a mesh axis runs over, the one named last changes fastest.
Arguments:
- eigvecs: bfloat16 [2, 2, 256, 3, 64, 256], P('tm', None, None, None, 'space'), may hold values from -6 to 6
- links: float32 [2, 3, 3, 3, 2, 64, 256], P('tm', None, None, None, None, 'space'), may hold values from -2.5 to 2.5
- momenta: int32 [4, 3], P('op'), may hold values from -2 to 2
- coef_num: int32 [4, 4, 3], P(None, 'op'), may hold values from -3 to 3
- coef_den: int32 [4], replicated, may hold values from 1 to 6
- peram: bfloat16 [2, 256, 4, 4, 2, 256], P('tm'), may hold values from -0.25 to 0.25
Outputs:
- quark_lines: float32 [2, 4, 4, 4, 2, 256, 256], P('tm', 'op', None, None, None, 'space')
The draws below stay inside these ranges and needn't reach their ends.
All inputs are finite; a program needn't handle non-finite values.
Results may differ from the reference program's by a relative error of at most 0.0053.
Values may be sent and summed in bfloat16 or wider, within the bound.
A program may use at most 128 MiB of HBM per device.

```python
import math
import jax
import jax.numpy as jnp
from jax import lax

NV = 256
LY = 32
LZ = 8
NMOM = 4
NDIR = 3
HEL = 4
NX = 64
PLANE = 256
NT = 2


def place_ends(drawn, rng, least, largest):
    longest = drawn.shape.index(max(drawn.shape))
    spots = []
    for shift in (0, 1):
        where = [jax.random.randint(jax.random.fold_in(rng, axis), (), 0, length) for axis, length in enumerate(drawn.shape)]
        where[longest] = (where[longest] + shift) % drawn.shape[longest]
        spots.append(tuple(where))
    return drawn.at[spots[0]].set(least).at[spots[1]].set(largest)


def level_of(own_key, extent, cuts, low, top_value):
    level, own = 1.0, jax.random.fold_in(own_key, 6)
    for position, blocks in cuts:
        heights = jnp.exp(jax.random.uniform(jax.random.fold_in(own, position), (blocks,), jnp.float32, low / len(cuts), top_value / len(cuts)))
        level = level * jnp.repeat(heights, extent[position] // blocks).reshape([-1 if axis == position else 1 for axis in range(len(extent))])
    return level


def centred(stream_key, extent, spread, limit, cuts=(), kind=jnp.bfloat16):
    loudness = level_of(stream_key, extent, cuts, -0.22, 0.18) if cuts else 1.0
    array = jax.random.normal(stream_key, extent, jnp.float32) * spread * loudness
    return jnp.minimum(jnp.maximum(array, -limit), limit).astype(kind)


def setup_inputs(seed: int = 0) -> dict:
    seeds = jax.random.split(jax.random.key(seed), 7)
    return {
        "eigvecs": centred(seeds[0], (NT, 2, NV, 3, NX, PLANE), 1.0, 6.0, ((0, 2), (4, 32))),
        "links": centred(seeds[1], (NT, NDIR, 3, 3, 2, NX, PLANE), 6 ** -0.5, 2.5, ((0, 2), (5, 32)), jnp.float32),
        "momenta": place_ends(jax.random.randint(seeds[2], (NMOM, 3), -2, 3), jax.random.fold_in(seeds[2], 1), -2, 2).astype(jnp.int32),
        "coef_num": place_ends(jax.random.randint(seeds[3], (HEL, NMOM, NDIR), -3, 4), jax.random.fold_in(seeds[3], 1), -3, 3).astype(jnp.int32),
        "coef_den": place_ends(jax.random.randint(seeds[4], (HEL,), 1, 7), jax.random.fold_in(seeds[4], 1), 1, 6).astype(jnp.int32),
        "peram": centred(seeds[5], (NT, NV, 4, 4, 2, NV), (2 * NV) ** -0.5, 0.25, ((0, 2),)),
    }


def colour(link, field, dagger):
    reals = []
    imags = []
    for col in range(3):
        acc_r = None
        acc_i = None
        for col_two in range(3):
            if dagger:
                link_r = link[col_two, col, 0]
                link_i = -link[col_two, col, 1]
            else:
                link_r = link[col, col_two, 0]
                link_i = link[col, col_two, 1]
            field_r = field[0, :, col_two].astype(jnp.float32)
            field_i = field[1, :, col_two].astype(jnp.float32)
            term_r = link_r * field_r - link_i * field_i
            term_i = link_r * field_i + link_i * field_r
            acc_r = term_r if acc_r is None else acc_r + term_r
            acc_i = term_i if acc_i is None else acc_i + term_i
        reals.append(acc_r)
        imags.append(acc_i)
    return jnp.stack([jnp.stack(reals, 1), jnp.stack(imags, 1)], 0)

def roll_plane(arr, by, axis):
    shape = arr.shape
    grid = arr.reshape(shape[:-1] + (LY, LZ))
    return jnp.roll(grid, by, axis=axis).reshape(shape)

def angles(mom, coord_x, n_x):
    yy = jnp.arange(LY, dtype=jnp.int32)
    zz = jnp.arange(LZ, dtype=jnp.int32)
    part_x = (mom[0] * coord_x % n_x).astype(jnp.float32) / n_x
    part_y = (mom[1] * yy % LY).astype(jnp.float32) / LY
    part_z = (mom[2] * zz % LZ).astype(jnp.float32) / LZ
    total = part_x[:, None, None] + part_y[None, :, None] + part_z[None, None, :]
    return (2.0 * math.pi * total).reshape(coord_x.shape[0], LY * LZ)

def left_operand(vec, theta):
    cosine = jnp.cos(theta)
    sine = jnp.sin(theta)
    vec_r = vec[0].astype(jnp.float32)
    vec_i = vec[1].astype(jnp.float32)
    left_r = cosine * vec_r - sine * vec_i
    left_i = -(sine * vec_r + cosine * vec_i)
    return jnp.stack([left_r, left_i], 0).astype(jnp.bfloat16)

def contract(left, right_mat, count):
    depth = right_mat.shape[1]
    mat = left.reshape(2 * count, depth)
    prod = lax.dot_general(mat, right_mat, (((1,), (1,)), ((), ())), preferred_element_type=jnp.float32)
    prod = prod.reshape(2, count, NDIR, 2, -1)
    real = prod[0, :, :, 0] - prod[1, :, :, 1]
    imag = prod[0, :, :, 1] + prod[1, :, :, 0]
    return jnp.stack([real, imag], 2)

def quark(ops_b, tau):
    hel_n, _, rows_n, cols_n = ops_b.shape
    left = ops_b.reshape(hel_n * 2 * rows_n, cols_n)
    right = tau.reshape(cols_n, -1)
    out = jnp.dot(left, right, preferred_element_type=jnp.float32)
    out = out.reshape(hel_n, 2, rows_n, 4, 4, 2, -1)
    real = out[:, 0, :, :, :, 0] - out[:, 1, :, :, :, 1]
    imag = out[:, 0, :, :, :, 1] + out[:, 1, :, :, :, 0]
    res = jnp.stack([real, imag], 4)
    return jnp.transpose(res, (0, 2, 3, 4, 1, 5))

def reference(eigvecs, links, momenta, coef_num, coef_den, peram):
    scale = 1.0 / math.sqrt(3.0 * NX * LY * LZ)
    weights = coef_num.astype(jnp.float32) / coef_den.astype(jnp.float32)[:, None, None]
    coord_x = jnp.arange(NX, dtype=jnp.int32)
    results = []
    for tslice in range(NT):
        vec = eigvecs[tslice]
        displaced = []
        for direc in range(NDIR):
            link = links[tslice, direc]
            back = colour(link, vec, True).astype(jnp.bfloat16)
            if direc == 0:
                vec_plus = jnp.roll(vec, -1, axis=3)
                back_minus = jnp.roll(back, 1, axis=3)
            else:
                vec_plus = roll_plane(vec, -1, direc + 3)
                back_minus = roll_plane(back, 1, direc + 3)
            forward = colour(link, vec_plus, False)
            displaced.append((forward - back_minus.astype(jnp.float32)).astype(jnp.bfloat16))
        right_mat = jnp.stack(displaced, 0).reshape(NDIR * 2 * NV, -1)
        elems = []
        for mom_idx in range(NMOM):
            theta = angles(momenta[mom_idx], coord_x, NX)
            left = left_operand(vec, theta)
            elems.append(contract(left, right_mat, NV) * scale)
        phi = jnp.stack(elems, 1)
        ops = jnp.einsum('hpd,apdrb->hrab', weights, phi, precision=lax.Precision.HIGHEST)
        ops_b = ops.astype(jnp.bfloat16)
        results.append(quark(ops_b, peram[1 - tslice]))
    return jnp.stack(results, 0)
```

```python
import functools
import math

import jax
import jax.numpy as jnp
from jax import lax
from jax.experimental import pallas as pl
from jax.experimental.pallas import tpu as pltpu
from jax.sharding import PartitionSpec as P

MESH = pl.DeviceIdType.MESH
F32 = jnp.float32
BF16 = jnp.bfloat16
NS = 32
NX = 64
LY = 32
LZ = 8
PL = LY * LZ
NV = 256
NB = NV // 2
HEL = 4
SCALE = 1.0 / math.sqrt(3.0 * NX * LY * LZ)
WROW = 108


def nt_dot(a, b):
    return lax.dot_general(a, b, (((1,), (1,)), ((), ())), preferred_element_type=F32)


def kernel(mom, num, den, lk, v2, piece, out,
           xp, xm, halo_l, wloc, wrem, bc, vs, perm, shf, dbuf, pbuf, rbuf, tbuf, sbuf, obuf,
           s_halo, r_up, r_dn, r_lk, s_w, r_w, s_z, r_z, s_g, r_g1, r_g2, r_sib, s_rs, r_rs, s_o, r_o):
    me = lax.axis_index("space")
    tm = lax.axis_index("tm")
    op = lax.axis_index("op")

    def dev(space, t, o):
        return {"space": space, "tm": t, "op": o}

    def plane_dev(space):
        return dev(space, tm, op)

    def remote(src, dst, ssem, rsem, where):
        return pltpu.make_async_remote_copy(src_ref=src, dst_ref=dst, send_sem=ssem, recv_sem=rsem,
                                            device_id=where, device_id_type=MESH)

    core = lax.rem(me, 2)
    chip = me // 2
    cx = chip // 4
    cy = lax.rem(chip, 4)
    sib = me + 1 - 2 * core
    nxt = lax.rem(me + 1, NS)
    prv = lax.rem(me + NS - 1, NS)

    barrier = pltpu.get_barrier_semaphore()

    @pl.loop(1, NS)
    def _(d):
        pl.semaphore_signal(barrier, inc=1, device_id=plane_dev(lax.rem(me + d, NS)), device_id_type=MESH)

    pl.semaphore_signal(barrier, inc=1, device_id=dev(me, tm, 1 - op), device_id_type=MESH)
    pl.semaphore_signal(barrier, inc=1, device_id=dev(me, 1 - tm, 1 - op), device_id_type=MESH)
    pl.semaphore_wait(barrier, NS + 1)

    z_copy = remote(piece, tbuf.at[me], s_z, r_z, dev(me, 1 - tm, 1 - op))
    z_copy.start()

    brow = pl.multiple_of(op * NB, NB)
    halo = []
    for f in range(6):
        ri, c = f // 3, f % 3
        rows = pl.ds(pl.multiple_of(ri * NV + brow, NB), NB)
        up = remote(v2.at[rows, pl.ds(c * 2 * PL, PL)], xp.at[f, :, pl.ds(PL, PL)],
                    s_halo.at[f], r_up.at[f], plane_dev(prv))
        dn = remote(v2.at[rows, pl.ds(c * 2 * PL + PL, PL)], xm.at[f, :, pl.ds(0, PL)],
                    s_halo.at[6 + f], r_dn.at[f], plane_dev(nxt))
        up.start()
        dn.start()
        halo += [up, dn]
    lk_copy = remote(lk.at[pl.ds(0, 18)], halo_l, s_halo.at[12], r_lk, plane_dev(nxt))
    lk_copy.start()
    halo.append(lk_copy)

    site = lax.broadcasted_iota(jnp.int32, (8, PL), 1)
    yy = site // LZ
    zz = lax.rem(site, LZ)
    inv = [SCALE / (jnp.zeros((8, PL), F32) + den[h].astype(F32)) for h in range(HEL)]
    for plane in range(2):
        phase = []
        for p in range(2):
            turn = (mom[p, 0] * (2 * me + plane)) & (NX - 1)
            turn = turn + 2 * ((mom[p, 1] * yy) & (LY - 1)) + 8 * ((mom[p, 2] * zz) & (LZ - 1))
            theta = (2.0 * math.pi / NX) * turn.astype(F32)
            phase.append((jnp.cos(theta), -jnp.sin(theta)))
        for h in range(HEL):
            for j in range(3):
                n0 = num[h, 0, j].astype(F32)
                n1 = num[h, 1, j].astype(F32)
                for ri in range(2):
                    w = (phase[0][ri] * n0 + phase[1][ri] * n1) * inv[h]
                    row = (h * 3 + j) * 2 + ri
                    wloc[plane, row:row + 1, :] = w[0:1]
    w_copy = remote(wloc, wrem, s_w, r_w, dev(me, tm, 1 - op))
    w_copy.start()

    for f in range(6):
        ri, c = f // 3, f % 3
        rows = pl.ds(pl.multiple_of(ri * NV + brow, NB), NB)
        p0 = v2[rows, c * 2 * PL:c * 2 * PL + PL]
        p1 = v2[rows, c * 2 * PL + PL:(c + 1) * 2 * PL]
        xp[f, :, 0:PL] = p1
        xm[f, :, PL:2 * PL] = p0
        vs[0, f * NB:(f + 1) * NB, :] = p0
        vs[1, f * NB:(f + 1) * NB, :] = p1
    r_i = lax.broadcasted_iota(jnp.int32, (PL, PL), 0)
    c_i = lax.broadcasted_iota(jnp.int32, (PL, PL), 1)
    zc = c_i & (LZ - 1)
    sources = [(c_i + LZ) & (PL - 1), (c_i - LZ) & (PL - 1),
               c_i - zc + ((zc + 1) & (LZ - 1)), c_i - zc + ((zc - 1) & (LZ - 1))]
    for q in range(4):
        perm[q] = jnp.where(r_i == sources[q], 1.0, 0.0).astype(BF16)
    for q in range(4):
        for plane in range(2):
            @pl.loop(0, 3)
            def _(m):
                rows = pl.ds(pl.multiple_of(m * 256, 256), 256)
                got = jnp.dot(vs[plane, rows, :], perm[q], preferred_element_type=F32)
                shf[q, rows, plane * PL:(plane + 1) * PL] = got

    lane_z = zz

    @pl.loop(0, 18)
    def _(k):
        for plane in range(2):
            for j in range(3):
                row = jnp.broadcast_to(lk[j * 18 + k, plane:plane + 1, :], (8, PL))
                if j == 1:
                    low = pltpu.roll(row, LZ, 1)
                elif j == 2:
                    low = jnp.where(lane_z == 0, pltpu.roll(row, PL - LZ + 1, 1), pltpu.roll(row, 1, 1))
                for lt in range(2):
                    sl = slice(lt * 128, lt * 128 + 128)
                    bc[plane * 2 + lt, j * 18 + k] = row[:, sl]
                    if j > 0:
                        bc[plane * 2 + lt, 54 + j * 18 + k] = low[:, sl]
                    elif plane == 0:
                        bc[2 + lt, 54 + k] = row[:, sl]

    z_copy.wait()
    st1 = 8 - 6 * core
    st2 = 2 + 6 * core
    p1 = cx * (1 - core) + cy * core
    p2 = cy * (1 - core) + cx * core

    def along(d, pos, stride):
        return me + (lax.rem(pos + d, 4) - pos) * stride

    gathers = []
    for d in range(1, 4):
        g = remote(tbuf.at[me], tbuf.at[me], s_g.at[d - 1], r_g1.at[d - 1], plane_dev(along(d, p1, st1)))
        g.start()
        gathers.append(g)
    sibs = [remote(tbuf.at[me], tbuf.at[me], s_g.at[15], r_sib, plane_dev(sib))]
    sibs[0].start()

    w_copy.wait()
    for plane in range(2):
        for r in range(24):
            w = jnp.broadcast_to(wloc[plane, r:r + 1, :] + wrem[plane, r:r + 1, :], (8, PL))
            for lt in range(2):
                bc[plane * 2 + lt, WROW + r] = w[:, lt * 128:lt * 128 + 128]

    for cp in halo:
        cp.wait()

    @pl.loop(0, 18)
    def _(k):
        row = jnp.broadcast_to(halo_l[k, 1:2, :], (8, PL))
        for lt in range(2):
            bc[lt, 54 + k] = row[:, lt * 128:lt * 128 + 128]

    def tile_work(t, vg):
        lanes = pl.ds(pl.multiple_of(t * 128, 128), 128)
        rows = pl.ds(pl.multiple_of(vg * 16, 16), 16)

        def field(j, back, f):
            if j == 0:
                ref = xm if back else xp
                return ref[f, rows, lanes].astype(F32).reshape(2, 8, 128)
            q = (j - 1) * 2 + back
            return shf[q, pl.ds(pl.multiple_of(f * NB + vg * 16, 16), 16), lanes].reshape(2, 8, 128)

        def coef(r):
            return bc[t, r][None]

        for c in range(3):
            acc = [[None, None] for _ in range(HEL)]
            for j in range(3):
                re = None
                im = None
                for c2 in range(3):
                    fr, fi = field(j, 0, c2), field(j, 0, 3 + c2)
                    gr, gi = field(j, 1, c2), field(j, 1, 3 + c2)
                    ur = coef(j * 18 + (c * 3 + c2) * 2)
                    ui = coef(j * 18 + (c * 3 + c2) * 2 + 1)
                    lr = coef(54 + j * 18 + (c2 * 3 + c) * 2)
                    li = coef(54 + j * 18 + (c2 * 3 + c) * 2 + 1)
                    a = ur * fr - ui * fi
                    b = ur * fi + ui * fr
                    a = a - lr * gr - li * gi
                    b = b - lr * gi + li * gr
                    re = a if re is None else re + a
                    im = b if im is None else im + b
                for h in range(HEL):
                    wr = coef(WROW + (h * 3 + j) * 2)
                    wi = coef(WROW + (h * 3 + j) * 2 + 1)
                    a = wr * re - wi * im
                    b = wr * im + wi * re
                    acc[h][0] = a if acc[h][0] is None else acc[h][0] + a
                    acc[h][1] = b if acc[h][1] is None else acc[h][1] + b
            cols = pl.ds(pl.multiple_of(c * 2 * PL + t * 128, 128), 128)
            for h in range(HEL):
                for ri in range(2):
                    dst = pl.ds(pl.multiple_of(ri * NB + vg * 16, 16), 16)
                    dbuf[h, dst, cols] = acc[h][ri].reshape(16, 128).astype(BF16)

    def run_tiles(t0, t1):
        @pl.loop(t0 * 8, t1 * 8)
        def _(i):
            tile_work(i // 8, lax.rem(i, 8))

    run_tiles(0, 2)

    for g in gathers:
        g.wait()
    second = []
    for a in range(4):
        k = along(a, p1, st1)
        for d in range(1, 4):
            where = k + (lax.rem(p2 + d, 4) - p2) * st2
            g = remote(tbuf.at[k], tbuf.at[k], s_g.at[3 + a * 3 + d - 1], r_g2.at[a * 3 + d - 1],
                       plane_dev(along(d, p2, st2)))
            del where
            g.start()
            second.append(g)
        if a > 0:
            s = remote(tbuf.at[k], tbuf.at[k], s_g.at[15], r_sib, plane_dev(sib))
            s.start()
            sibs.append(s)

    run_tiles(2, 4)

    @pl.loop(0, HEL)
    def _(h):
        full = nt_dot(v2[...], dbuf[h])
        re = full[:NV, :NB] + full[NV:, NB:]
        im = full[:NV, NB:] - full[NV:, :NB]
        pbuf[:, h, 0] = re.reshape(NS, 8, NB)
        pbuf[:, h, 1] = im.reshape(NS, 8, NB)

        @pl.loop(1, NS)
        def _(d):
            owner = lax.rem(me + d, NS)
            remote(pbuf.at[owner, h], rbuf.at[d - 1, h], s_rs, r_rs, plane_dev(owner)).start()

    for g in second:
        g.wait()
    for a in range(4):
        for d in range(1, 4):
            k = along(a, p1, st1) + (lax.rem(p2 + 4 - d, 4) - p2) * st2
            s = remote(tbuf.at[k], tbuf.at[k], s_g.at[15], r_sib, plane_dev(sib))
            s.start()
            sibs.append(s)

    whole = remote(pbuf.at[pl.ds(0, NS - 1)], rbuf, s_rs, r_rs, plane_dev(nxt))
    whole.wait_recv()

    def add(d, acc):
        return acc + rbuf[d]

    total = lax.fori_loop(0, NS - 1, add, pbuf[me])
    sbuf[...] = total.reshape(HEL, 16, NB).astype(BF16)
    mine = pl.ds(2 * op, 2)
    theirs = pl.ds(2 * (1 - op), 2)
    cols = pl.ds(pl.multiple_of(op * NB, NB), NB)
    o_copy = remote(sbuf.at[theirs], obuf.at[:, :, cols], s_o, r_o, dev(me, tm, 1 - op))
    o_copy.start()
    obuf[:, :, cols] = sbuf[mine]
    whole.wait_send()
    o_copy.wait()

    parity = remote(tbuf.at[pl.ds(0, 16)], tbuf.at[pl.ds(0, 16)], s_g.at[15], r_sib, plane_dev(sib))
    parity.wait()

    ops = obuf[...].astype(F32)
    lines = []
    for h in range(2):
        o_r, o_i = ops[h, 0:8], ops[h, 8:16]
        lines.append(jnp.concatenate([o_r, -o_i], 1))
        lines.append(jnp.concatenate([o_i, o_r], 1))
    left = jnp.concatenate(lines, 0).astype(BF16)

    @pl.loop(0, 16)
    def _(g):
        right = jnp.concatenate([tbuf[2 * g], tbuf[2 * g + 1]], 1)
        res = jnp.dot(left, right, preferred_element_type=F32)
        out[:, g] = res.reshape(2, 2, 8, NV)


def shards(eigvecs, links, momenta, coef_num, coef_den, peram):
    v2 = eigvecs[0].reshape(2 * NV, 3 * 2 * PL)
    lk = links[0].reshape(54, 2, PL)
    me = lax.axis_index("space")
    per = peram[0].reshape(NV, 16, 2, NV)
    piece = lax.dynamic_slice(per, (0, me // 2, 0, (me % 2) * 128), (NV, 1, 2, 128))
    piece = jnp.transpose(piece[:, 0], (1, 0, 2)).reshape(2 * NV, 128)
    vm = pl.BlockSpec(memory_space=pltpu.VMEM)
    sm = pl.BlockSpec(memory_space=pltpu.SMEM)
    dma = pltpu.SemaphoreType.DMA
    out = pl.pallas_call(
        kernel,
        out_shape=jax.ShapeDtypeStruct((2, 16, 2, 8, NV), F32),
        in_specs=[sm, sm, sm, vm, vm, vm],
        out_specs=vm,
        scratch_shapes=[
            pltpu.VMEM((6, NB, 2 * PL), BF16),
            pltpu.VMEM((6, NB, 2 * PL), BF16),
            pltpu.VMEM((18, 2, PL), F32),
            pltpu.VMEM((2, 24, PL), F32),
            pltpu.VMEM((2, 24, PL), F32),
            pltpu.VMEM((4, 132, 8, 128), F32),
            pltpu.VMEM((2, 6 * NB, PL), BF16),
            pltpu.VMEM((4, PL, PL), BF16),
            pltpu.VMEM((4, 6 * NB, 2 * PL), F32),
            pltpu.VMEM((HEL, NV, 6 * PL), BF16),
            pltpu.VMEM((NS, HEL, 2, 8, NB), F32),
            pltpu.VMEM((NS - 1, HEL, 2, 8, NB), F32),
            pltpu.VMEM((NS, 2 * NV, 128), BF16),
            pltpu.VMEM((HEL, 16, NB), BF16),
            pltpu.VMEM((2, 16, NV), BF16),
            dma((13,)), dma((6,)), dma((6,)), dma, dma, dma, dma, dma,
            dma((16,)), dma((3,)), dma((12,)), dma, dma, dma, dma, dma,
        ],
        compiler_params=pltpu.CompilerParams(collective_id=0, has_side_effects=True,
                                             vmem_limit_bytes=60 * 1024 * 1024),
    )(momenta, coef_num, coef_den, lk, v2, piece)
    return out.reshape(1, 2, 4, 4, 2, 8, NV)


def solution(mesh):
    return jax.shard_map(
        shards,
        mesh=mesh,
        in_specs=(
            P("tm", None, None, None, "space", None),
            P("tm", None, None, None, None, "space", None),
            P("op", None),
            P(None, "op", None),
            P(),
            P("tm", None, None, None, None, None),
        ),
        out_specs=P("tm", "op", None, None, None, "space", None),
        check_vma=False,
    )
```

```python
import functools
import math

import jax
import jax.numpy as jnp
from jax import lax
from jax.experimental import pallas as pl
from jax.experimental.pallas import tpu as pltpu
from jax.sharding import PartitionSpec as P

MESH = pl.DeviceIdType.MESH
F32 = jnp.float32
BF16 = jnp.bfloat16
NS = 32
NX = 64
LY = 32
LZ = 8
PL = LY * LZ
NV = 256
NB = NV // 2
HEL = 4
SCALE = 1.0 / math.sqrt(3.0 * NX * LY * LZ)
WROW = 108


def nt_dot(a, b):
    return lax.dot_general(a, b, (((1,), (1,)), ((), ())), preferred_element_type=F32)


def kernel(mom, num, den, lk, v, piece, out,
           xp, xm, halo_l, wloc, wrem, bc, vs, perm, shf, dbuf, pbuf, rbuf, tbuf, sbuf, obuf,
           s_halo, r_up, r_dn, r_lk, s_w, r_w, s_z, r_z, s_g, r_g1, r_g2, s_sib, r_sib, s_rs, r_rs, s_o, r_o):
    me = lax.axis_index("space")
    tm = lax.axis_index("tm")
    op = lax.axis_index("op")

    def dev(space, t, o):
        return {"space": space, "tm": t, "op": o}

    def plane_dev(space):
        return dev(space, tm, op)

    def remote(src, dst, ssem, rsem, where):
        return pltpu.make_async_remote_copy(src_ref=src, dst_ref=dst, send_sem=ssem, recv_sem=rsem,
                                            device_id=where, device_id_type=MESH)

    core = lax.rem(me, 2)
    chip = me // 2
    cx = chip // 4
    cy = lax.rem(chip, 4)
    sib = me + 1 - 2 * core
    nxt = lax.rem(me + 1, NS)
    prv = lax.rem(me + NS - 1, NS)

    st1 = 8 - 6 * core
    st2 = 2 + 6 * core
    p1 = cx * (1 - core) + cy * core
    p2 = cy * (1 - core) + cx * core
    LOW, HIGH, ALL = pl.ds(0, NV), pl.ds(NV, NV), pl.ds(0, 2 * NV)

    def move1(s, d):
        return s + (lax.rem(p1 + d, 4) - p1) * st1

    def move2(s, d):
        return s + (lax.rem(p2 + d, 4) - p2) * st2

    def held(s, o):
        return move2(s, 2 * o)

    right1, left1 = move1(me, 1), move1(me, 3)
    right2, left2 = move2(me, 1), move2(me, 3)

    barrier = pltpu.get_barrier_semaphore()

    @pl.loop(1, NS)
    def _(d):
        pl.semaphore_signal(barrier, inc=1, device_id=plane_dev(lax.rem(me + d, NS)), device_id_type=MESH)

    pl.semaphore_signal(barrier, inc=1, device_id=dev(me, tm, 1 - op), device_id_type=MESH)
    pl.semaphore_signal(barrier, inc=1, device_id=dev(me, 1 - tm, 1 - op), device_id_type=MESH)

    site = lax.broadcasted_iota(jnp.int32, (8, PL), 1)
    yy = site // LZ
    zz = site & (LZ - 1)
    inv = [SCALE / (jnp.zeros((8, PL), F32) + den[h].astype(F32)) for h in range(HEL)]
    for plane in range(2):
        phase = []
        for p in range(2):
            turn = (mom[p, 0] * (2 * me + plane)) & (NX - 1)
            turn = turn + 2 * ((mom[p, 1] * yy) & (LY - 1)) + 8 * ((mom[p, 2] * zz) & (LZ - 1))
            theta = (2.0 * math.pi / NX) * turn.astype(F32)
            phase.append((jnp.cos(theta), -jnp.sin(theta)))
        for h in range(HEL):
            for j in range(3):
                n0 = num[j, 0, h].astype(F32)
                n1 = num[j, 1, h].astype(F32)
                for ri in range(2):
                    w = (phase[0][ri] * n0 + phase[1][ri] * n1) * inv[h]
                    row = (h * 3 + j) * 2 + ri
                    wloc[plane, row:row + 1, :] = w[0:1]

    pl.semaphore_wait(barrier, NS + 1)

    z_copy = remote(piece, tbuf.at[held(me, 1 - op)], s_z, r_z, dev(me, 1 - tm, 1 - op))
    came = held(me, op)
    z_copy.start()

    brow = pl.ds(pl.multiple_of(op * NB, NB), NB)
    halo = []
    for f in range(6):
        ri, c = f // 3, f % 3
        up = remote(v.at[c, 0, ri, brow], xp.at[f, :, pl.ds(PL, PL)],
                    s_halo.at[f], r_up.at[f], plane_dev(prv))
        dn = remote(v.at[c, 1, ri, brow], xm.at[f, :, pl.ds(0, PL)],
                    s_halo.at[6 + f], r_dn.at[f], plane_dev(nxt))
        up.start()
        dn.start()
        halo += [up, dn]
    lk_copy = remote(lk.at[pl.ds(0, 18)], halo_l, s_halo.at[12], r_lk, plane_dev(nxt))
    lk_copy.start()
    halo.append(lk_copy)
    w_copy = remote(wloc, wrem, s_w, r_w, dev(me, tm, 1 - op))
    w_copy.start()

    for f in range(6):
        ri, c = f // 3, f % 3
        even = v[c, 0, ri, brow]
        odd = v[c, 1, ri, brow]
        xp[f, :, 0:PL] = odd
        xm[f, :, PL:2 * PL] = even
        vs[0, f * NB:(f + 1) * NB, :] = even
        vs[1, f * NB:(f + 1) * NB, :] = odd
    r_i = lax.broadcasted_iota(jnp.int32, (PL, PL), 0)
    c_i = lax.broadcasted_iota(jnp.int32, (PL, PL), 1)
    zc = c_i & (LZ - 1)
    sources = [(c_i + LZ) & (PL - 1), (c_i - LZ) & (PL - 1),
               c_i - zc + ((zc + 1) & (LZ - 1)), c_i - zc + ((zc - 1) & (LZ - 1))]
    for q in range(4):
        perm[q] = jnp.where(r_i == sources[q], 1.0, 0.0).astype(BF16)
    for q in range(4):
        for plane in range(2):
            shf[q, :, plane * PL:(plane + 1) * PL] = jnp.dot(vs[plane], perm[q], preferred_element_type=F32)

    z_copy.wait()
    def send(k, part, n, rsem, where):
        ref = tbuf.at[k, part]
        g = remote(ref, ref, s_g.at[n], rsem, plane_dev(where))
        g.start()
        return g

    def to_sibling(k):
        ref = tbuf.at[k]
        remote(ref, ref, s_sib, r_sib, plane_dev(sib)).start()

    def spread(k, n):
        ahead.append((send(k, ALL, 4 + 2 * n, r_g2.at[2 * n], right2),
                      send(k, ALL, 5 + 2 * n, r_g2.at[2 * n + 1], left2)))
        ref = tbuf.at[k]
        g = remote(ref, ref, s_g.at[12 + n], r_g2.at[8 + n], dev(me, tm, 1 - op))
        g.start()
        across.append(g)
        to_sibling(k)

    ahead = []
    across = []
    first = [send(came, ALL, 0, r_g1.at[0], right1), send(came, ALL, 1, r_g1.at[1], left1)]
    spread(came, 0)

    @pl.loop(0, 18)
    def _(k):
        for plane in range(2):
            for j in range(3):
                row = jnp.broadcast_to(lk[j * 18 + k, plane:plane + 1, :], (8, PL))
                if j == 1:
                    low = pltpu.roll(row, LZ, 1)
                elif j == 2:
                    low = jnp.where(zz == 0, pltpu.roll(row, PL - LZ + 1, 1), pltpu.roll(row, 1, 1))
                for lt in range(2):
                    sl = slice(lt * 128, lt * 128 + 128)
                    bc[plane * 2 + lt, j * 18 + k] = row[:, sl]
                    if j > 0:
                        bc[plane * 2 + lt, 54 + j * 18 + k] = low[:, sl]
                    elif plane == 0:
                        bc[2 + lt, 54 + k] = row[:, sl]

    w_copy.wait()
    for plane in range(2):
        for r in range(24):
            w = jnp.broadcast_to(wloc[plane, r:r + 1, :] + wrem[plane, r:r + 1, :], (8, PL))
            for lt in range(2):
                bc[plane * 2 + lt, WROW + r] = w[:, lt * 128:lt * 128 + 128]

    for cp in halo:
        cp.wait()

    @pl.loop(0, 18)
    def _(k):
        row = jnp.broadcast_to(halo_l[k, 1:2, :], (8, PL))
        for lt in range(2):
            bc[lt, 54 + k] = row[:, lt * 128:lt * 128 + 128]

    def tile_work(t, vg):
        lanes = pl.ds(pl.multiple_of(t * 128, 128), 128)
        rows = pl.ds(pl.multiple_of(vg * 16, 16), 16)

        def field(j, back, f):
            if j == 0:
                ref = xm if back else xp
                return ref[f, rows, lanes].astype(F32).reshape(2, 8, 128)
            q = (j - 1) * 2 + back
            return shf[q, pl.ds(pl.multiple_of(f * NB + vg * 16, 16), 16), lanes].reshape(2, 8, 128)

        def coef(r):
            return bc[t, r][None]

        for c in range(3):
            acc = [[None, None] for _ in range(HEL)]
            for j in range(3):
                re = None
                im = None
                for c2 in range(3):
                    fr, fi = field(j, 0, c2), field(j, 0, 3 + c2)
                    gr, gi = field(j, 1, c2), field(j, 1, 3 + c2)
                    ur = coef(j * 18 + (c * 3 + c2) * 2)
                    ui = coef(j * 18 + (c * 3 + c2) * 2 + 1)
                    lr = coef(54 + j * 18 + (c2 * 3 + c) * 2)
                    li = coef(54 + j * 18 + (c2 * 3 + c) * 2 + 1)
                    a = ur * fr - ui * fi
                    b = ur * fi + ui * fr
                    a = a - lr * gr - li * gi
                    b = b - lr * gi + li * gr
                    re = a if re is None else re + a
                    im = b if im is None else im + b
                for h in range(HEL):
                    wr = coef(WROW + (h * 3 + j) * 2)
                    wi = coef(WROW + (h * 3 + j) * 2 + 1)
                    a = wr * re - wi * im
                    b = wr * im + wi * re
                    acc[h][0] = a if acc[h][0] is None else acc[h][0] + a
                    acc[h][1] = b if acc[h][1] is None else acc[h][1] + b
            cols = pl.ds(pl.multiple_of(c * 2 * PL + t * 128, 128), 128)
            for h in range(HEL):
                for ri in range(2):
                    dst = pl.ds(pl.multiple_of(ri * NB + vg * 16, 16), 16)
                    dbuf[h, dst, cols] = acc[h][ri].reshape(16, 128).astype(BF16)

    def run_tiles(i0, i1):
        @pl.loop(i0, i1)
        def _(i):
            tile_work(i // 8, lax.rem(i, 8))

    run_tiles(0, 8)

    for g in first:
        g.wait()
    kl, kr, ko = move1(came, 3), move1(came, 1), move1(came, 2)
    onward = [send(kl, LOW, 2, r_g1.at[2], right1), send(kr, HIGH, 3, r_g1.at[3], left1)]
    spread(kl, 1)
    spread(kr, 2)

    run_tiles(8, 16)

    for g in onward:
        g.wait()
    spread(ko, 3)

    run_tiles(16, 24)

    def settle(n):
        for g in ahead[n]:
            g.wait()
        across[n].wait()
        k = (came, kl, kr, ko)[n]
        to_sibling(turned(k, 3))
        to_sibling(turned(k, 1))
        to_sibling(turned(k, 2))

    def turned(k, d):
        at = lax.rem(p2 + 2 * op, 4)
        return k + (lax.rem(at + d, 4) - at) * st2

    settle(0)
    run_tiles(24, 32)

    @pl.loop(0, HEL)
    def _(h):
        full = None
        for cp in range(6):
            part = nt_dot(v[cp // 2, cp % 2].reshape(2 * NV, PL), dbuf[h, :, cp * PL:(cp + 1) * PL])
            full = part if full is None else full + part
        re = full[:NV, :NB] + full[NV:, NB:]
        im = full[:NV, NB:] - full[NV:, :NB]
        both = jnp.concatenate([re.reshape(NS, 8, NB), im.reshape(NS, 8, NB)], 1)
        pbuf[:, h] = both.astype(BF16)

        @pl.loop(1, NS)
        def _(d):
            owner = lax.rem(me + d, NS)
            remote(pbuf.at[owner, h], rbuf.at[d - 1, h], s_rs, r_rs, plane_dev(owner)).start()

    for n in range(1, 4):
        settle(n)

    whole = remote(pbuf.at[pl.ds(0, NS - 1)], rbuf, s_rs, r_rs, plane_dev(nxt))
    whole.wait_recv()

    def add(d, acc):
        return acc + rbuf[d].astype(F32)

    total = lax.fori_loop(0, NS - 1, add, pbuf[me].astype(F32))
    sbuf[...] = total.astype(BF16)
    mine = pl.ds(2 * op, 2)
    theirs = pl.ds(2 * (1 - op), 2)
    cols = pl.ds(pl.multiple_of(op * NB, NB), NB)
    o_copy = remote(sbuf.at[theirs], obuf.at[:, :, cols], s_o, r_o, dev(me, tm, 1 - op))
    o_copy.start()
    obuf[:, :, cols] = sbuf[mine]
    whole.wait_send()
    o_copy.wait()

    half = tbuf.at[pl.ds(0, 16)]
    remote(half, half, s_sib, r_sib, plane_dev(sib)).wait()

    ops = obuf[...].astype(F32)
    lines = []
    for h in range(2):
        o_r, o_i = ops[h, 0:8], ops[h, 8:16]
        lines.append(jnp.concatenate([o_r, -o_i], 1))
        lines.append(jnp.concatenate([o_i, o_r], 1))
    left = jnp.concatenate(lines, 0).astype(BF16)

    @pl.loop(0, 16)
    def _(g):
        right = jnp.concatenate([tbuf[2 * g], tbuf[2 * g + 1]], 1)
        res = jnp.dot(left, right, preferred_element_type=F32)
        out[:, g] = res.reshape(2, 2, 8, NV)


def shards(eigvecs, links, momenta, coef_num, coef_den, peram):
    v = jnp.transpose(eigvecs[0], (2, 3, 0, 1, 4))
    lk = links[0].reshape(54, 2, PL)
    me = lax.axis_index("space")
    core = me % 2
    row = 2 * lax.axis_index("op")
    cx, cy = me // 8, (me // 2) % 4
    row = 2 - row
    place = jnp.where(core == 0, cx * 4 + (cy + row) % 4, (cx + row) % 4 * 4 + cy)
    per = peram[0].reshape(NV, 16, 2, NV)
    piece = lax.dynamic_slice(per, (0, place, 0, core * 128), (NV, 1, 2, 128))
    piece = jnp.transpose(piece[:, 0], (1, 0, 2)).reshape(2 * NV, 128)
    vm = pl.BlockSpec(memory_space=pltpu.VMEM)
    sm = pl.BlockSpec(memory_space=pltpu.SMEM)
    dma = pltpu.SemaphoreType.DMA
    out = pl.pallas_call(
        kernel,
        out_shape=jax.ShapeDtypeStruct((2, 16, 2, 8, NV), F32),
        in_specs=[sm, sm, sm, vm, vm, vm],
        out_specs=vm,
        scratch_shapes=[
            pltpu.VMEM((6, NB, 2 * PL), BF16),
            pltpu.VMEM((6, NB, 2 * PL), BF16),
            pltpu.VMEM((18, 2, PL), F32),
            pltpu.VMEM((2, 24, PL), F32),
            pltpu.VMEM((2, 24, PL), F32),
            pltpu.VMEM((4, 132, 8, 128), F32),
            pltpu.VMEM((2, 6 * NB, PL), BF16),
            pltpu.VMEM((4, PL, PL), BF16),
            pltpu.VMEM((4, 6 * NB, 2 * PL), F32),
            pltpu.VMEM((HEL, NV, 6 * PL), BF16),
            pltpu.VMEM((NS, HEL, 16, NB), BF16),
            pltpu.VMEM((NS - 1, HEL, 16, NB), BF16),
            pltpu.VMEM((NS, 2 * NV, 128), BF16),
            pltpu.VMEM((HEL, 16, NB), BF16),
            pltpu.VMEM((2, 16, NV), BF16),
            dma((13,)), dma((6,)), dma((6,)), dma, dma, dma, dma, dma,
            dma((20,)), dma((4,)), dma((16,)), dma, dma, dma, dma, dma, dma,
        ],
        compiler_params=pltpu.CompilerParams(collective_id=0, has_side_effects=True,
                                             vmem_limit_bytes=60 * 1024 * 1024),
    )(momenta, jnp.transpose(coef_num, (2, 1, 0)), coef_den, lk, v, piece)
    return out.reshape(1, 2, 4, 4, 2, 8, NV)


def solution(mesh):
    return jax.shard_map(
        shards,
        mesh=mesh,
        in_specs=(
            P("tm", None, None, None, "space", None),
            P("tm", None, None, None, None, "space", None),
            P("op", None),
            P(None, "op", None),
            P(),
            P("tm", None, None, None, None, None),
        ),
        out_specs=P("tm", "op", None, None, None, "space", None),
        check_vma=False,
    )
```

```python
import functools
import math

import jax
import jax.numpy as jnp
from jax import lax
from jax.experimental import pallas as pl
from jax.experimental.pallas import tpu as pltpu
from jax.sharding import PartitionSpec as P

MESH = pl.DeviceIdType.MESH
F32 = jnp.float32
BF16 = jnp.bfloat16
NS = 32
NX = 64
LY = 32
LZ = 8
PL = LY * LZ
NV = 256
NB = NV // 2
HEL = 4
SCALE = 1.0 / math.sqrt(3.0 * NX * LY * LZ)
WROW = 108


def nt_dot(a, b):
    return lax.dot_general(a, b, (((1,), (1,)), ((), ())), preferred_element_type=F32)


def kernel(mom, num, den, lk, v, piece, out,
           xp, xm, halo_l, wloc, wrem, bc, vs, perm, shf, part, dbuf, pf, pq, ps, pbuf, rbuf, tbuf, sbuf, obuf,
           s_halo, r_up, r_dn, r_lk, s_w, r_w, s_z, r_z, s_g, r_g1, r_g2, s_sib, r_sib, s_ps, r_ps, s_rs, r_rs, s_o, r_o):
    me = lax.axis_index("space")
    tm = lax.axis_index("tm")
    op = lax.axis_index("op")

    def dev(space, t, o):
        return {"space": space, "tm": t, "op": o}

    def plane_dev(space):
        return dev(space, tm, op)

    def remote(src, dst, ssem, rsem, where):
        return pltpu.make_async_remote_copy(src_ref=src, dst_ref=dst, send_sem=ssem, recv_sem=rsem,
                                            device_id=where, device_id_type=MESH)

    core = lax.rem(me, 2)
    chip = me // 2
    cx = chip // 4
    cy = lax.rem(chip, 4)
    sib = me + 1 - 2 * core
    nxt = lax.rem(me + 1, NS)
    prv = lax.rem(me + NS - 1, NS)

    st1 = 8 - 6 * core
    st2 = 2 + 6 * core
    p1 = cx * (1 - core) + cy * core
    p2 = cy * (1 - core) + cx * core
    LOW, HIGH, ALL = pl.ds(0, NV), pl.ds(NV, NV), pl.ds(0, 2 * NV)

    def move1(s, d):
        return s + (lax.rem(p1 + d, 4) - p1) * st1

    def move2(s, d):
        return s + (lax.rem(p2 + d, 4) - p2) * st2

    def held(s, o):
        return move2(s, 2 * o)

    right1, left1 = move1(me, 1), move1(me, 3)
    right2, left2 = move2(me, 1), move2(me, 3)

    barrier = pltpu.get_barrier_semaphore()

    def same_core(d):
        return lax.rem(chip + d, NS // 2) * 2 + core

    @pl.loop(1, NS // 2)
    def _(d):
        pl.semaphore_signal(barrier, inc=1, device_id=plane_dev(same_core(d)), device_id_type=MESH)

    cross = lax.rem(me + NS + 2 * core - 1, NS)
    for where in (plane_dev(cross), plane_dev(sib), dev(me, tm, 1 - op), dev(me, 1 - tm, 1 - op)):
        pl.semaphore_signal(barrier, inc=1, device_id=where, device_id_type=MESH)

    site = lax.broadcasted_iota(jnp.int32, (8, PL), 1)
    yy = site // LZ
    zz = site & (LZ - 1)
    inv = [SCALE / (jnp.zeros((8, PL), F32) + den[h].astype(F32)) for h in range(HEL)]
    for plane in range(2):
        phase = []
        for p in range(2):
            turn = (mom[p, 0] * (2 * me + plane)) & (NX - 1)
            turn = turn + 2 * ((mom[p, 1] * yy) & (LY - 1)) + 8 * ((mom[p, 2] * zz) & (LZ - 1))
            theta = (2.0 * math.pi / NX) * turn.astype(F32)
            phase.append((jnp.cos(theta), -jnp.sin(theta)))
        for h in range(HEL):
            for j in range(3):
                n0 = num[j, 0, h].astype(F32)
                n1 = num[j, 1, h].astype(F32)
                for ri in range(2):
                    w = (phase[0][ri] * n0 + phase[1][ri] * n1) * inv[h]
                    row = (h * 3 + j) * 2 + ri
                    wloc[plane, row:row + 1, :] = w[0:1]

    pl.semaphore_wait(barrier, NS // 2 + 3)

    brow = pl.ds(pl.multiple_of(op * NB, NB), NB)
    halo = []
    for f in range(6):
        ri, c = f // 3, f % 3
        up = remote(v.at[c, 0, ri, brow], xp.at[f, :, pl.ds(PL, PL)],
                    s_halo.at[f], r_up.at[f], plane_dev(prv))
        dn = remote(v.at[c, 1, ri, brow], xm.at[f, :, pl.ds(0, PL)],
                    s_halo.at[6 + f], r_dn.at[f], plane_dev(nxt))
        up.start()
        dn.start()
        halo += [up, dn]
    lk_copy = remote(lk.at[pl.ds(0, 18)], halo_l, s_halo.at[12], r_lk, plane_dev(nxt))
    lk_copy.start()
    halo.append(lk_copy)
    w_copy = remote(wloc, wrem, s_w, r_w, dev(me, tm, 1 - op))
    w_copy.start()

    z_copy = remote(piece, tbuf.at[held(me, 1 - op)], s_z, r_z, dev(me, 1 - tm, 1 - op))
    came = held(me, op)
    z_copy.start()

    for f in range(6):
        ri, c = f // 3, f % 3
        even = v[c, 0, ri, brow]
        odd = v[c, 1, ri, brow]
        xp[f, :, 0:PL] = odd
        xm[f, :, PL:2 * PL] = even
        vs[0, f * NB:(f + 1) * NB, :] = even
        vs[1, f * NB:(f + 1) * NB, :] = odd
    r_i = lax.broadcasted_iota(jnp.int32, (PL, PL), 0)
    c_i = lax.broadcasted_iota(jnp.int32, (PL, PL), 1)
    zc = c_i & (LZ - 1)
    sources = [(c_i + LZ) & (PL - 1), (c_i - LZ) & (PL - 1),
               c_i - zc + ((zc + 1) & (LZ - 1)), c_i - zc + ((zc - 1) & (LZ - 1))]
    for q in range(4):
        perm[q] = jnp.where(r_i == sources[q], 1.0, 0.0).astype(BF16)
    for q in range(4):
        for plane in range(2):
            shf[q, :, plane * PL:(plane + 1) * PL] = jnp.dot(vs[plane], perm[q], preferred_element_type=F32)

    @pl.loop(0, 18)
    def _(k):
        for plane in range(2):
            for j in range(3):
                row = jnp.broadcast_to(lk[j * 18 + k, plane:plane + 1, :], (8, PL))
                if j == 1:
                    low = pltpu.roll(row, LZ, 1)
                elif j == 2:
                    low = jnp.where(zz == 0, pltpu.roll(row, PL - LZ + 1, 1), pltpu.roll(row, 1, 1))
                for lt in range(2):
                    sl = slice(lt * 128, lt * 128 + 128)
                    bc[plane * 2 + lt, j * 18 + k] = row[:, sl]
                    if j > 0:
                        bc[plane * 2 + lt, 54 + j * 18 + k] = low[:, sl]
                    elif plane == 0:
                        bc[2 + lt, 54 + k] = row[:, sl]

    w_copy.wait()
    for plane in range(2):
        for r in range(24):
            w = jnp.broadcast_to(wloc[plane, r:r + 1, :] + wrem[plane, r:r + 1, :], (8, PL))
            for lt in range(2):
                bc[plane * 2 + lt, WROW + r] = w[:, lt * 128:lt * 128 + 128]

    def tile_work(i, dirs, load, store):
        half = i // 16
        t = lax.rem(i, 16) // 4
        quarter = lax.rem(i, 4)
        vg = half * 4 + quarter
        lanes = pl.ds(pl.multiple_of(t * 128, 128), 128)
        rows = pl.ds(pl.multiple_of(vg * 16, 16), 16)

        def field(j, back, f):
            if j == 0:
                ref = xm if back else xp
                return ref[f, rows, lanes].astype(F32).reshape(2, 8, 128)
            q = (j - 1) * 2 + back
            return shf[q, pl.ds(pl.multiple_of(f * NB + vg * 16, 16), 16), lanes].reshape(2, 8, 128)

        def coef(r):
            return bc[t, r][None]

        for c in range(3):
            acc = [[None, None] for _ in range(HEL)]
            if load:
                acc = [[part[i, (c * HEL + h) * 2 + ri] for ri in range(2)] for h in range(HEL)]
            for j in dirs:
                re = None
                im = None
                for c2 in range(3):
                    fr, fi = field(j, 0, c2), field(j, 0, 3 + c2)
                    gr, gi = field(j, 1, c2), field(j, 1, 3 + c2)
                    ur = coef(j * 18 + (c * 3 + c2) * 2)
                    ui = coef(j * 18 + (c * 3 + c2) * 2 + 1)
                    lr = coef(54 + j * 18 + (c2 * 3 + c) * 2)
                    li = coef(54 + j * 18 + (c2 * 3 + c) * 2 + 1)
                    a = ur * fr - ui * fi
                    b = ur * fi + ui * fr
                    a = a - lr * gr - li * gi
                    b = b - lr * gi + li * gr
                    re = a if re is None else re + a
                    im = b if im is None else im + b
                for h in range(HEL):
                    wr = coef(WROW + (h * 3 + j) * 2)
                    wi = coef(WROW + (h * 3 + j) * 2 + 1)
                    a = wr * re - wi * im
                    b = wr * im + wi * re
                    acc[h][0] = a if acc[h][0] is None else acc[h][0] + a
                    acc[h][1] = b if acc[h][1] is None else acc[h][1] + b
            if not store:
                for h in range(HEL):
                    for ri in range(2):
                        part[i, (c * HEL + h) * 2 + ri] = acc[h][ri]
                continue
            cols = pl.ds(pl.multiple_of(c * 2 * PL + t * 128, 128), 128)
            for h in range(HEL):
                for ri in range(2):
                    dst = pl.ds(pl.multiple_of(ri * NB + h % 2 * (NB // 2) + quarter * 16, 16), 16)
                    dbuf[half, h // 2, dst, cols] = acc[h][ri].reshape(16, 128).astype(BF16)

    def run_tiles(i0, i1, dirs=(0, 1, 2), load=False, store=True):
        @pl.loop(i0, i1)
        def _(i):
            tile_work(i, dirs, load, store)

    def send(k, part, n, rsem, where):
        ref = tbuf.at[k, part]
        g = remote(ref, ref, s_g.at[n], rsem, plane_dev(where))
        g.start()
        return g

    def to_sibling(k):
        ref = tbuf.at[k]
        remote(ref, ref, s_sib, r_sib, plane_dev(sib)).start()

    def spread(k, n):
        ahead.append((send(k, ALL, 4 + 2 * n, r_g2.at[2 * n], right2),
                      send(k, ALL, 5 + 2 * n, r_g2.at[2 * n + 1], left2)))
        ref = tbuf.at[k]
        g = remote(ref, ref, s_g.at[12 + n], r_g2.at[8 + n], dev(me, tm, 1 - op))
        g.start()
        across.append(g)
        to_sibling(k)

    EARLY = 16
    run_tiles(0, EARLY // 2, (1, 2), False, False)

    z_copy.wait()
    ahead = []
    across = []
    first = [send(came, ALL, 0, r_g1.at[0], right1), send(came, ALL, 1, r_g1.at[1], left1)]
    spread(came, 0)

    run_tiles(EARLY // 2, EARLY, (1, 2), False, False)

    for cp in halo:
        cp.wait()

    @pl.loop(0, 18)
    def _(k):
        row = jnp.broadcast_to(halo_l[k, 1:2, :], (8, PL))
        for lt in range(2):
            bc[lt, 54 + k] = row[:, lt * 128:lt * 128 + 128]

    run_tiles(0, EARLY, (0,), True, True)

    def products(half):
        for hp in range(2):
            full = None
            for cp in range(6):
                prod = nt_dot(v[cp // 2, cp % 2].reshape(2 * NV, PL), dbuf[half, hp, :, cp * PL:(cp + 1) * PL])
                full = prod if full is None else full + prod
            re = full[:NV, :NB] + full[NV:, NB:]
            im = full[:NV, NB:] - full[NV:, :NB]
            pf[half, hp, :, :, 0:8] = re.reshape(NS // 2, 2, 8, NB)
            pf[half, hp, :, :, 8:16] = im.reshape(NS // 2, 2, 8, NB)
            pq[half, hp] = pf[half, hp, :, 1 - core].astype(BF16)
        g = remote(pq.at[half], ps.at[half], s_ps.at[half], r_ps.at[half], plane_dev(sib))
        g.start()
        return g

    def combine(half, g):
        g.wait()
        for hp in range(2):
            pbuf[:, 2 * half + hp] = (pf[half, hp, :, core] + ps[half, hp].astype(F32)).astype(BF16)

        @pl.loop(1, NS // 2)
        def _(d):
            owner = lax.rem(chip + d, NS // 2)
            remote(pbuf.at[owner, pl.ds(2 * half, 2)], rbuf.at[d - 1, pl.ds(2 * half, 2)], s_rs, r_rs,
                   plane_dev(owner * 2 + core)).start()

    early = products(0)

    for g in first:
        g.wait()
    kl, kr, ko = move1(came, 3), move1(came, 1), move1(came, 2)
    onward = [send(kl, LOW, 2, r_g1.at[2], right1), send(kr, HIGH, 3, r_g1.at[3], left1)]
    spread(kl, 1)
    spread(kr, 2)

    run_tiles(EARLY, 22)
    combine(0, early)
    run_tiles(22, 27)

    for g in onward:
        g.wait()
    spread(ko, 3)

    def turned(k, d):
        at = lax.rem(p2 + 2 * op, 4)
        return k + (lax.rem(at + d, 4) - at) * st2

    def settle(n):
        for g in ahead[n]:
            g.wait()
        across[n].wait()
        k = (came, kl, kr, ko)[n]
        to_sibling(turned(k, 3))
        to_sibling(turned(k, 1))
        to_sibling(turned(k, 2))

    run_tiles(27, 32)
    combine(1, products(1))

    for n in range(4):
        settle(n)

    whole = remote(pbuf.at[pl.ds(0, NS // 2 - 1)], rbuf, s_rs, r_rs, plane_dev(sib))
    whole.wait_recv()

    def add(d, acc):
        return acc + rbuf[d].astype(F32)

    own = pf[:, :, chip, core] + ps[:, :, chip].astype(F32)
    total = lax.fori_loop(0, NS // 2 - 1, add, own.reshape(4, 16, NB))
    sbuf[...] = total.reshape(2, 2, 16, NB).astype(BF16)
    o_copy = remote(sbuf.at[:, 1 - op], obuf.at[op], s_o, r_o, dev(me, tm, 1 - op))
    o_copy.start()
    obuf[op] = sbuf[:, op]
    whole.wait_send()
    o_copy.wait()

    half = tbuf.at[pl.ds(0, 16)]
    remote(half, half, s_sib, r_sib, plane_dev(sib)).wait()

    lane = lax.broadcasted_iota(jnp.int32, (16, NB), 1)
    low = lane < NB // 2
    rows = [[], []]
    for o in range(2):
        a, b = obuf[o, 0].astype(F32), obuf[o, 1].astype(F32)
        rows[0].append(jnp.where(low, a, pltpu.roll(b, NB // 2, 1)))
        rows[1].append(jnp.where(low, pltpu.roll(a, NB // 2, 1), b))
    lines = []
    for h in range(2):
        ops = jnp.concatenate(rows[h], 1)
        o_r, o_i = ops[0:8], ops[8:16]
        lines.append(jnp.concatenate([o_r, -o_i], 1))
        lines.append(jnp.concatenate([o_i, o_r], 1))
    left = jnp.concatenate(lines, 0).astype(BF16)

    @pl.loop(0, 4)
    def _(q):
        for n in range(4):
            g = 4 * q + n
            right = jnp.concatenate([tbuf[2 * g], tbuf[2 * g + 1]], 1)
            res = jnp.dot(left, right, preferred_element_type=F32)
            out[:, g] = res.reshape(2, 2, 8, NV)


def shards(eigvecs, links, momenta, coef_num, coef_den, peram):
    v = jnp.transpose(eigvecs[0], (2, 3, 0, 1, 4))
    lk = links[0].reshape(54, 2, PL)
    me = lax.axis_index("space")
    core = me % 2
    row = 2 * lax.axis_index("op")
    cx, cy = me // 8, (me // 2) % 4
    row = 2 - row
    place = jnp.where(core == 0, cx * 4 + (cy + row) % 4, (cx + row) % 4 * 4 + cy)
    per = peram[0].reshape(NV, 16, 2, NV)
    piece = lax.dynamic_slice(per, (0, place, 0, core * 128), (NV, 1, 2, 128))
    piece = jnp.transpose(piece[:, 0], (1, 0, 2)).reshape(2 * NV, 128)
    vm = pl.BlockSpec(memory_space=pltpu.VMEM)
    sm = pl.BlockSpec(memory_space=pltpu.SMEM)
    dma = pltpu.SemaphoreType.DMA
    out = pl.pallas_call(
        kernel,
        out_shape=jax.ShapeDtypeStruct((2, 16, 2, 8, NV), F32),
        in_specs=[sm, sm, sm, vm, vm, vm],
        out_specs=vm,
        scratch_shapes=[
            pltpu.VMEM((6, NB, 2 * PL), BF16),
            pltpu.VMEM((6, NB, 2 * PL), BF16),
            pltpu.VMEM((18, 2, PL), F32),
            pltpu.VMEM((2, 24, PL), F32),
            pltpu.VMEM((2, 24, PL), F32),
            pltpu.VMEM((4, 132, 8, 128), F32),
            pltpu.VMEM((2, 6 * NB, PL), BF16),
            pltpu.VMEM((4, PL, PL), BF16),
            pltpu.VMEM((4, 6 * NB, 2 * PL), F32),
            pltpu.VMEM((16, 24, 2, 8, 128), F32),
            pltpu.VMEM((2, 2, NV, 6 * PL), BF16),
            pltpu.VMEM((2, 2, NS // 2, 2, 16, NB), F32),
            pltpu.VMEM((2, 2, NS // 2, 16, NB), BF16),
            pltpu.VMEM((2, 2, NS // 2, 16, NB), BF16),
            pltpu.VMEM((NS // 2, HEL, 16, NB), BF16),
            pltpu.VMEM((NS // 2 - 1, HEL, 16, NB), BF16),
            pltpu.VMEM((NS, 2 * NV, 128), BF16),
            pltpu.VMEM((2, 2, 16, NB), BF16),
            pltpu.VMEM((2, 2, 16, NB), BF16),
            dma((13,)), dma((6,)), dma((6,)), dma, dma, dma, dma, dma,
            dma((20,)), dma((4,)), dma((16,)), dma, dma, dma((2,)), dma((2,)), dma, dma, dma, dma,
        ],
        compiler_params=pltpu.CompilerParams(collective_id=0, has_side_effects=True,
                                             vmem_limit_bytes=48 * 1024 * 1024),
    )(momenta, jnp.transpose(coef_num, (2, 1, 0)), coef_den, lk, v, piece)
    return out.reshape(1, 2, 4, 4, 2, 8, NV)


def solution(mesh):
    return jax.shard_map(
        shards,
        mesh=mesh,
        in_specs=(
            P("tm", None, None, None, "space", None),
            P("tm", None, None, None, None, "space", None),
            P("op", None),
            P(None, "op", None),
            P(),
            P("tm", None, None, None, None, None),
        ),
        out_specs=P("tm", "op", None, None, None, "space", None),
        check_vma=False,
    )
```

```python
import functools
import math

import jax
import jax.numpy as jnp
from jax import lax
from jax.experimental import pallas as pl
from jax.experimental.pallas import tpu as pltpu
from jax.sharding import PartitionSpec as P

MESH = pl.DeviceIdType.MESH
F32 = jnp.float32
BF16 = jnp.bfloat16
NS = 32
NX = 64
LY = 32
LZ = 8
PL = LY * LZ
NV = 256
NB = NV // 2
HEL = 4
SCALE = 1.0 / math.sqrt(3.0 * NX * LY * LZ)
WROW = 108


def nt_dot(a, b):
    return lax.dot_general(a, b, (((1,), (1,)), ((), ())), preferred_element_type=F32)


def kernel(mom_h, num_h, den_h, lk_h, v, piece, out,
           mom, num, den, lk, s_in, xp, xm, halo_l, wloc, wrem, bc, vs, perm, shf, part, dbuf, pf, pq, ps, pbuf, rbuf, tbuf, sbuf, obuf,
           s_halo, r_up, r_dn, r_lk, s_w, r_w, s_z, r_z, s_g, r_g1, r_g2, s_sib, r_sib, s_ps, r_ps, s_rs, r_rs, s_o, r_o):
    me = lax.axis_index("space")
    tm = lax.axis_index("tm")
    op = lax.axis_index("op")

    def dev(space, t, o):
        return {"space": space, "tm": t, "op": o}

    def plane_dev(space):
        return dev(space, tm, op)

    def remote(src, dst, ssem, rsem, where):
        return pltpu.make_async_remote_copy(src_ref=src, dst_ref=dst, send_sem=ssem, recv_sem=rsem,
                                            device_id=where, device_id_type=MESH)

    core = lax.rem(me, 2)
    chip = me // 2
    cx = chip // 4
    cy = lax.rem(chip, 4)
    sib = me + 1 - 2 * core
    nxt = lax.rem(me + 1, NS)
    prv = lax.rem(me + NS - 1, NS)

    st1 = 8 - 6 * core
    st2 = 2 + 6 * core
    p1 = cx * (1 - core) + cy * core
    p2 = cy * (1 - core) + cx * core
    LOW, HIGH, ALL = pl.ds(0, NV), pl.ds(NV, NV), pl.ds(0, 2 * NV)

    def move1(s, d):
        return s + (lax.rem(p1 + d, 4) - p1) * st1

    def move2(s, d):
        return s + (lax.rem(p2 + d, 4) - p2) * st2

    def held(s, o):
        return move2(s, 2 * o)

    right1, left1 = move1(me, 1), move1(me, 3)
    right2, left2 = move2(me, 1), move2(me, 3)

    fetches = [pltpu.make_async_copy(a, b, s_in.at[n])
               for n, (a, b) in enumerate(((mom_h, mom), (num_h, num), (den_h, den), (lk_h, lk)))]
    for cp in fetches:
        cp.start()

    barrier = pltpu.get_barrier_semaphore()

    def same_core(d):
        return lax.rem(chip + d, NS // 2) * 2 + core

    @pl.loop(1, NS // 2)
    def _(d):
        pl.semaphore_signal(barrier, inc=1, device_id=plane_dev(same_core(d)), device_id_type=MESH)

    cross = lax.rem(me + NS + 2 * core - 1, NS)
    for where in (plane_dev(cross), plane_dev(sib), dev(me, tm, 1 - op), dev(me, 1 - tm, 1 - op)):
        pl.semaphore_signal(barrier, inc=1, device_id=where, device_id_type=MESH)

    for cp in fetches[:3]:
        cp.wait()
    site = lax.broadcasted_iota(jnp.int32, (8, PL), 1)
    yy = site // LZ
    zz = site & (LZ - 1)
    inv = [SCALE / (jnp.zeros((8, PL), F32) + den[h].astype(F32)) for h in range(HEL)]
    for plane in range(2):
        phase = []
        for p in range(2):
            turn = (mom[p, 0] * (2 * me + plane)) & (NX - 1)
            turn = turn + 2 * ((mom[p, 1] * yy) & (LY - 1)) + 8 * ((mom[p, 2] * zz) & (LZ - 1))
            theta = (2.0 * math.pi / NX) * turn.astype(F32)
            phase.append((jnp.cos(theta), -jnp.sin(theta)))
        for h in range(HEL):
            for j in range(3):
                n0 = num[j, 0, h].astype(F32)
                n1 = num[j, 1, h].astype(F32)
                for ri in range(2):
                    w = (phase[0][ri] * n0 + phase[1][ri] * n1) * inv[h]
                    row = (h * 3 + j) * 2 + ri
                    wloc[plane, row:row + 1, :] = w[0:1]

    pl.semaphore_wait(barrier, NS // 2 + 3)

    brow = pl.ds(pl.multiple_of(op * NB, NB), NB)
    halo = []
    for f in range(6):
        ri, c = f // 3, f % 3
        up = remote(v.at[c, 0, ri, brow], xp.at[f, :, pl.ds(PL, PL)],
                    s_halo.at[f], r_up.at[f], plane_dev(prv))
        dn = remote(v.at[c, 1, ri, brow], xm.at[f, :, pl.ds(0, PL)],
                    s_halo.at[6 + f], r_dn.at[f], plane_dev(nxt))
        up.start()
        dn.start()
        halo += [up, dn]
    lk_copy = remote(lk_h.at[pl.ds(0, 18)], halo_l, s_halo.at[12], r_lk, plane_dev(nxt))
    lk_copy.start()
    halo.append(lk_copy)
    w_copy = remote(wloc, wrem, s_w, r_w, dev(me, tm, 1 - op))
    w_copy.start()

    z_copy = remote(piece, tbuf.at[held(me, 1 - op)], s_z, r_z, dev(me, 1 - tm, 1 - op))
    came = held(me, op)
    z_copy.start()

    for f in range(6):
        ri, c = f // 3, f % 3
        even = v[c, 0, ri, brow]
        odd = v[c, 1, ri, brow]
        xp[f, :, 0:PL] = odd
        xm[f, :, PL:2 * PL] = even
        vs[0, f * NB:(f + 1) * NB, :] = even
        vs[1, f * NB:(f + 1) * NB, :] = odd
    r_i = lax.broadcasted_iota(jnp.int32, (PL, PL), 0)
    c_i = lax.broadcasted_iota(jnp.int32, (PL, PL), 1)
    zc = c_i & (LZ - 1)
    sources = [(c_i + LZ) & (PL - 1), (c_i - LZ) & (PL - 1),
               c_i - zc + ((zc + 1) & (LZ - 1)), c_i - zc + ((zc - 1) & (LZ - 1))]
    for q in range(4):
        perm[q] = jnp.where(r_i == sources[q], 1.0, 0.0).astype(BF16)
    for q in range(4):
        for plane in range(2):
            shf[q, :, plane * PL:(plane + 1) * PL] = jnp.dot(vs[plane], perm[q], preferred_element_type=F32)

    fetches[3].wait()

    @pl.loop(0, 18)
    def _(k):
        for plane in range(2):
            for j in range(3):
                row = jnp.broadcast_to(lk[j * 18 + k, plane:plane + 1, :], (8, PL))
                if j == 1:
                    low = pltpu.roll(row, LZ, 1)
                elif j == 2:
                    low = jnp.where(zz == 0, pltpu.roll(row, PL - LZ + 1, 1), pltpu.roll(row, 1, 1))
                for lt in range(2):
                    sl = slice(lt * 128, lt * 128 + 128)
                    bc[plane * 2 + lt, j * 18 + k] = row[:, sl]
                    if j > 0:
                        bc[plane * 2 + lt, 54 + j * 18 + k] = low[:, sl]
                    elif plane == 0:
                        bc[2 + lt, 54 + k] = row[:, sl]

    w_copy.wait()
    for plane in range(2):
        for r in range(24):
            w = jnp.broadcast_to(wloc[plane, r:r + 1, :] + wrem[plane, r:r + 1, :], (8, PL))
            for lt in range(2):
                bc[plane * 2 + lt, WROW + r] = w[:, lt * 128:lt * 128 + 128]

    def tile_work(i, dirs, load, store):
        half = i // 16
        t = lax.rem(i, 16) // 4
        quarter = lax.rem(i, 4)
        vg = half * 4 + quarter
        lanes = pl.ds(pl.multiple_of(t * 128, 128), 128)
        rows = pl.ds(pl.multiple_of(vg * 16, 16), 16)

        def field(j, back, f):
            if j == 0:
                ref = xm if back else xp
                return ref[f, rows, lanes].astype(F32).reshape(2, 8, 128)
            q = (j - 1) * 2 + back
            return shf[q, pl.ds(pl.multiple_of(f * NB + vg * 16, 16), 16), lanes].reshape(2, 8, 128)

        def coef(r):
            return bc[t, r][None]

        for c in range(3):
            acc = [[None, None] for _ in range(HEL)]
            if load:
                acc = [[part[i, (c * HEL + h) * 2 + ri] for ri in range(2)] for h in range(HEL)]
            for j in dirs:
                re = None
                im = None
                for c2 in range(3):
                    fr, fi = field(j, 0, c2), field(j, 0, 3 + c2)
                    gr, gi = field(j, 1, c2), field(j, 1, 3 + c2)
                    ur = coef(j * 18 + (c * 3 + c2) * 2)
                    ui = coef(j * 18 + (c * 3 + c2) * 2 + 1)
                    lr = coef(54 + j * 18 + (c2 * 3 + c) * 2)
                    li = coef(54 + j * 18 + (c2 * 3 + c) * 2 + 1)
                    a = ur * fr - ui * fi
                    b = ur * fi + ui * fr
                    a = a - lr * gr - li * gi
                    b = b - lr * gi + li * gr
                    re = a if re is None else re + a
                    im = b if im is None else im + b
                for h in range(HEL):
                    wr = coef(WROW + (h * 3 + j) * 2)
                    wi = coef(WROW + (h * 3 + j) * 2 + 1)
                    a = wr * re - wi * im
                    b = wr * im + wi * re
                    acc[h][0] = a if acc[h][0] is None else acc[h][0] + a
                    acc[h][1] = b if acc[h][1] is None else acc[h][1] + b
            if not store:
                for h in range(HEL):
                    for ri in range(2):
                        part[i, (c * HEL + h) * 2 + ri] = acc[h][ri]
                continue
            cols = pl.ds(pl.multiple_of(c * 2 * PL + t * 128, 128), 128)
            for h in range(HEL):
                for ri in range(2):
                    dst = pl.ds(pl.multiple_of(ri * NB + h % 2 * (NB // 2) + quarter * 16, 16), 16)
                    dbuf[half, h // 2, dst, cols] = acc[h][ri].reshape(16, 128).astype(BF16)

    def run_tiles(i0, i1, dirs=(0, 1, 2), load=False, store=True):
        @pl.loop(i0, i1)
        def _(i):
            tile_work(i, dirs, load, store)

    def send(k, part, n, rsem, where):
        ref = tbuf.at[k, part]
        g = remote(ref, ref, s_g.at[n], rsem, plane_dev(where))
        g.start()
        return g

    def to_sibling(k):
        ref = tbuf.at[k]
        remote(ref, ref, s_sib, r_sib, plane_dev(sib)).start()

    def spread(k, n):
        ahead.append((send(k, ALL, 4 + 2 * n, r_g2.at[2 * n], right2),
                      send(k, ALL, 5 + 2 * n, r_g2.at[2 * n + 1], left2)))
        ref = tbuf.at[k]
        g = remote(ref, ref, s_g.at[12 + n], r_g2.at[8 + n], dev(me, tm, 1 - op))
        g.start()
        across.append(g)
        to_sibling(k)

    EARLY = 16
    run_tiles(0, EARLY // 2, (1, 2), False, False)

    z_copy.wait()
    ahead = []
    across = []
    first = [send(came, ALL, 0, r_g1.at[0], right1), send(came, ALL, 1, r_g1.at[1], left1)]
    spread(came, 0)

    run_tiles(EARLY // 2, EARLY, (1, 2), False, False)

    for cp in halo:
        cp.wait()

    @pl.loop(0, 18)
    def _(k):
        row = jnp.broadcast_to(halo_l[k, 1:2, :], (8, PL))
        for lt in range(2):
            bc[lt, 54 + k] = row[:, lt * 128:lt * 128 + 128]

    run_tiles(0, EARLY, (0,), True, True)

    def products(half):
        for hp in range(2):
            full = None
            for cp in range(6):
                prod = nt_dot(v[cp // 2, cp % 2].reshape(2 * NV, PL), dbuf[half, hp, :, cp * PL:(cp + 1) * PL])
                full = prod if full is None else full + prod
            re = full[:NV, :NB] + full[NV:, NB:]
            im = full[:NV, NB:] - full[NV:, :NB]
            pf[half, hp, :, :, 0:8] = re.reshape(NS // 2, 2, 8, NB)
            pf[half, hp, :, :, 8:16] = im.reshape(NS // 2, 2, 8, NB)
            pq[half, hp] = pf[half, hp, :, 1 - core].astype(BF16)
        g = remote(pq.at[half], ps.at[half], s_ps.at[half], r_ps.at[half], plane_dev(sib))
        g.start()
        return g

    def combine(half, g):
        g.wait()
        for hp in range(2):
            pbuf[:, 2 * half + hp] = (pf[half, hp, :, core] + ps[half, hp].astype(F32)).astype(BF16)

        @pl.loop(1, NS // 2)
        def _(d):
            owner = lax.rem(chip + d, NS // 2)
            remote(pbuf.at[owner, pl.ds(2 * half, 2)], rbuf.at[d - 1, pl.ds(2 * half, 2)], s_rs, r_rs,
                   plane_dev(owner * 2 + core)).start()

    early = products(0)

    for g in first:
        g.wait()
    kl, kr, ko = move1(came, 3), move1(came, 1), move1(came, 2)
    onward = [send(kl, LOW, 2, r_g1.at[2], right1), send(kr, HIGH, 3, r_g1.at[3], left1)]
    spread(kl, 1)
    spread(kr, 2)

    run_tiles(EARLY, 22)
    combine(0, early)
    run_tiles(22, 27)

    for g in onward:
        g.wait()
    spread(ko, 3)

    def turned(k, d):
        at = lax.rem(p2 + 2 * op, 4)
        return k + (lax.rem(at + d, 4) - at) * st2

    def settle(n):
        for g in ahead[n]:
            g.wait()
        across[n].wait()
        k = (came, kl, kr, ko)[n]
        to_sibling(turned(k, 3))
        to_sibling(turned(k, 1))
        to_sibling(turned(k, 2))

    run_tiles(27, 32)
    combine(1, products(1))

    for n in range(4):
        settle(n)

    whole = remote(pbuf.at[pl.ds(0, NS // 2 - 1)], rbuf, s_rs, r_rs, plane_dev(sib))
    whole.wait_recv()

    def add(d, acc):
        return acc + rbuf[d].astype(F32)

    own = pf[:, :, chip, core] + ps[:, :, chip].astype(F32)
    total = lax.fori_loop(0, NS // 2 - 1, add, own.reshape(4, 16, NB))
    sbuf[...] = total.reshape(2, 2, 16, NB).astype(BF16)
    o_copy = remote(sbuf.at[:, 1 - op], obuf.at[op], s_o, r_o, dev(me, tm, 1 - op))
    o_copy.start()
    obuf[op] = sbuf[:, op]
    whole.wait_send()
    o_copy.wait()

    half = tbuf.at[pl.ds(0, 16)]
    remote(half, half, s_sib, r_sib, plane_dev(sib)).wait()

    lane = lax.broadcasted_iota(jnp.int32, (16, NB), 1)
    low = lane < NB // 2
    rows = [[], []]
    for o in range(2):
        a, b = obuf[o, 0].astype(F32), obuf[o, 1].astype(F32)
        rows[0].append(jnp.where(low, a, pltpu.roll(b, NB // 2, 1)))
        rows[1].append(jnp.where(low, pltpu.roll(a, NB // 2, 1), b))
    lines = []
    for h in range(2):
        ops = jnp.concatenate(rows[h], 1)
        o_r, o_i = ops[0:8], ops[8:16]
        lines.append(jnp.concatenate([o_r, -o_i], 1))
        lines.append(jnp.concatenate([o_i, o_r], 1))
    left = jnp.concatenate(lines, 0).astype(BF16)

    @pl.loop(0, 4)
    def _(q):
        for n in range(4):
            g = 4 * q + n
            right = jnp.concatenate([tbuf[2 * g], tbuf[2 * g + 1]], 1)
            res = jnp.dot(left, right, preferred_element_type=F32)
            out[:, g] = res.reshape(2, 2, 8, NV)


def shards(eigvecs, links, momenta, coef_num, coef_den, peram):
    v = jnp.transpose(eigvecs[0], (2, 3, 0, 1, 4))
    lk = links[0].reshape(54, 2, PL)
    me = lax.axis_index("space")
    core = me % 2
    row = 2 * lax.axis_index("op")
    cx, cy = me // 8, (me // 2) % 4
    row = 2 - row
    place = jnp.where(core == 0, cx * 4 + (cy + row) % 4, (cx + row) % 4 * 4 + cy)
    per = peram[0].reshape(NV, 16, 2, NV)
    piece = lax.dynamic_slice(per, (0, place, 0, core * 128), (NV, 1, 2, 128))
    piece = jnp.transpose(piece[:, 0], (1, 0, 2)).reshape(2 * NV, 128)
    hb = lambda x: pltpu.with_memory_space_constraint(x, pltpu.MemorySpace.HBM)
    vm = pl.BlockSpec(memory_space=pltpu.VMEM)
    hbm = pl.BlockSpec(memory_space=pltpu.MemorySpace.HBM)
    dma = pltpu.SemaphoreType.DMA
    out = pl.pallas_call(
        kernel,
        out_shape=jax.ShapeDtypeStruct((2, 16, 2, 8, NV), F32),
        in_specs=[hbm, hbm, hbm, hbm, vm, vm],
        out_specs=vm,
        scratch_shapes=[
            pltpu.SMEM((2, 3), jnp.int32),
            pltpu.SMEM((3, 2, HEL), jnp.int32),
            pltpu.SMEM((HEL,), jnp.int32),
            pltpu.VMEM((54, 2, PL), F32),
            dma((4,)),
            pltpu.VMEM((6, NB, 2 * PL), BF16),
            pltpu.VMEM((6, NB, 2 * PL), BF16),
            pltpu.VMEM((18, 2, PL), F32),
            pltpu.VMEM((2, 24, PL), F32),
            pltpu.VMEM((2, 24, PL), F32),
            pltpu.VMEM((4, 132, 8, 128), F32),
            pltpu.VMEM((2, 6 * NB, PL), BF16),
            pltpu.VMEM((4, PL, PL), BF16),
            pltpu.VMEM((4, 6 * NB, 2 * PL), F32),
            pltpu.VMEM((16, 24, 2, 8, 128), F32),
            pltpu.VMEM((2, 2, NV, 6 * PL), BF16),
            pltpu.VMEM((2, 2, NS // 2, 2, 16, NB), F32),
            pltpu.VMEM((2, 2, NS // 2, 16, NB), BF16),
            pltpu.VMEM((2, 2, NS // 2, 16, NB), BF16),
            pltpu.VMEM((NS // 2, HEL, 16, NB), BF16),
            pltpu.VMEM((NS // 2 - 1, HEL, 16, NB), BF16),
            pltpu.VMEM((NS, 2 * NV, 128), BF16),
            pltpu.VMEM((2, 2, 16, NB), BF16),
            pltpu.VMEM((2, 2, 16, NB), BF16),
            dma((13,)), dma((6,)), dma((6,)), dma, dma, dma, dma, dma,
            dma((20,)), dma((4,)), dma((16,)), dma, dma, dma((2,)), dma((2,)), dma, dma, dma, dma,
        ],
        compiler_params=pltpu.CompilerParams(collective_id=0, has_side_effects=True,
                                             vmem_limit_bytes=48 * 1024 * 1024),
    )(hb(momenta), hb(jnp.transpose(coef_num, (2, 1, 0))), hb(coef_den), hb(lk), v, piece)
    return out.reshape(1, 2, 4, 4, 2, 8, NV)


def solution(mesh):
    return jax.shard_map(
        shards,
        mesh=mesh,
        in_specs=(
            P("tm", None, None, None, "space", None),
            P("tm", None, None, None, None, "space", None),
            P("op", None),
            P(None, "op", None),
            P(),
            P("tm", None, None, None, None, None),
        ),
        out_specs=P("tm", "op", None, None, None, "space", None),
        check_vma=False,
    )
```

```python
import functools
import math

import jax
import jax.numpy as jnp
from jax import lax
from jax.experimental import pallas as pl
from jax.experimental.pallas import tpu as pltpu
from jax.sharding import PartitionSpec as P

MESH = pl.DeviceIdType.MESH
F32 = jnp.float32
BF16 = jnp.bfloat16
NS = 32
NX = 64
LY = 32
LZ = 8
PL = LY * LZ
NV = 256
NB = NV // 2
HEL = 4
SCALE = 1.0 / math.sqrt(3.0 * NX * LY * LZ)
WROW = 108


def nt_dot(a, b):
    return lax.dot_general(a, b, (((1,), (1,)), ((), ())), preferred_element_type=F32)


def kernel(mom_h, num_h, den_h, lk_h, v, piece, out,
           mom, num, den, lk, s_in, xp, xm, halo_l, wloc, wrem, bc, vs, perm, shf, part, dbuf, pf, pq, ps, pbuf, rbuf, tbuf, obuf,
           s_halo, r_up, r_dn, r_lk, s_w, r_w, s_z, r_z, s_g, r_g1, r_g2, s_sib, r_sib, s_ps, r_ps, s_rs, r_rs):
    me = lax.axis_index("space")
    tm = lax.axis_index("tm")
    op = lax.axis_index("op")

    def dev(space, t, o):
        return {"space": space, "tm": t, "op": o}

    def plane_dev(space):
        return dev(space, tm, op)

    def remote(src, dst, ssem, rsem, where):
        return pltpu.make_async_remote_copy(src_ref=src, dst_ref=dst, send_sem=ssem, recv_sem=rsem,
                                            device_id=where, device_id_type=MESH)

    core = lax.rem(me, 2)
    chip = me // 2
    cx = chip // 4
    cy = lax.rem(chip, 4)
    sib = me + 1 - 2 * core
    nxt = lax.rem(me + 1, NS)
    prv = lax.rem(me + NS - 1, NS)

    st1 = 8 - 6 * core
    st2 = 2 + 6 * core
    p1 = cx * (1 - core) + cy * core
    p2 = cy * (1 - core) + cx * core
    LOW, HIGH, ALL = pl.ds(0, NV), pl.ds(NV, NV), pl.ds(0, 2 * NV)

    def move1(s, d):
        return s + (lax.rem(p1 + d, 4) - p1) * st1

    def move2(s, d):
        return s + (lax.rem(p2 + d, 4) - p2) * st2

    def held(s, o):
        return move2(s, 2 * o)

    right1, left1 = move1(me, 1), move1(me, 3)
    right2, left2 = move2(me, 1), move2(me, 3)

    fetches = [pltpu.make_async_copy(a, b, s_in.at[n])
               for n, (a, b) in enumerate(((mom_h, mom), (num_h, num), (den_h, den), (lk_h, lk)))]
    for cp in fetches:
        cp.start()

    barrier = pltpu.get_barrier_semaphore()

    def same_core(d):
        return lax.rem(chip + d, NS // 2) * 2 + core

    @pl.loop(1, NS // 2)
    def _(d):
        pl.semaphore_signal(barrier, inc=1, device_id=plane_dev(same_core(d)), device_id_type=MESH)

    @pl.loop(0, NS // 2)
    def _(d):
        pl.semaphore_signal(barrier, inc=1, device_id=dev(same_core(d), tm, 1 - op), device_id_type=MESH)

    cross = lax.rem(me + NS + 2 * core - 1, NS)
    for where in (plane_dev(cross), plane_dev(sib), dev(me, 1 - tm, 1 - op)):
        pl.semaphore_signal(barrier, inc=1, device_id=where, device_id_type=MESH)

    for cp in fetches[:3]:
        cp.wait()
    site = lax.broadcasted_iota(jnp.int32, (8, PL), 1)
    yy = site // LZ
    zz = site & (LZ - 1)
    inv = [SCALE / (jnp.zeros((8, PL), F32) + den[h].astype(F32)) for h in range(HEL)]
    for plane in range(2):
        phase = []
        for p in range(2):
            turn = (mom[p, 0] * (2 * me + plane)) & (NX - 1)
            turn = turn + 2 * ((mom[p, 1] * yy) & (LY - 1)) + 8 * ((mom[p, 2] * zz) & (LZ - 1))
            theta = (2.0 * math.pi / NX) * turn.astype(F32)
            phase.append((jnp.cos(theta), -jnp.sin(theta)))
        for h in range(HEL):
            for j in range(3):
                n0 = num[j, 0, h].astype(F32)
                n1 = num[j, 1, h].astype(F32)
                for ri in range(2):
                    w = (phase[0][ri] * n0 + phase[1][ri] * n1) * inv[h]
                    row = (h * 3 + j) * 2 + ri
                    wloc[plane, row:row + 1, :] = w[0:1]

    pl.semaphore_wait(barrier, NS + 2)

    brow = pl.ds(pl.multiple_of(op * NB, NB), NB)
    halo = []
    for f in range(6):
        ri, c = f // 3, f % 3
        up = remote(v.at[c, 0, ri, brow], xp.at[f, :, pl.ds(PL, PL)],
                    s_halo.at[f], r_up.at[f], plane_dev(prv))
        dn = remote(v.at[c, 1, ri, brow], xm.at[f, :, pl.ds(0, PL)],
                    s_halo.at[6 + f], r_dn.at[f], plane_dev(nxt))
        up.start()
        dn.start()
        halo += [up, dn]
    lk_copy = remote(lk_h.at[pl.ds(0, 18)], halo_l, s_halo.at[12], r_lk, plane_dev(nxt))
    lk_copy.start()
    halo.append(lk_copy)
    w_copy = remote(wloc, wrem, s_w, r_w, dev(me, tm, 1 - op))
    w_copy.start()

    z_copy = remote(piece, tbuf.at[held(me, 1 - op)], s_z, r_z, dev(me, 1 - tm, 1 - op))
    came = held(me, op)
    z_copy.start()

    for f in range(6):
        ri, c = f // 3, f % 3
        even = v[c, 0, ri, brow]
        odd = v[c, 1, ri, brow]
        xp[f, :, 0:PL] = odd
        xm[f, :, PL:2 * PL] = even
        vs[0, f * NB:(f + 1) * NB, :] = even
        vs[1, f * NB:(f + 1) * NB, :] = odd
    r_i = lax.broadcasted_iota(jnp.int32, (PL, PL), 0)
    c_i = lax.broadcasted_iota(jnp.int32, (PL, PL), 1)
    zc = c_i & (LZ - 1)
    sources = [(c_i + LZ) & (PL - 1), (c_i - LZ) & (PL - 1),
               c_i - zc + ((zc + 1) & (LZ - 1)), c_i - zc + ((zc - 1) & (LZ - 1))]
    for q in range(4):
        perm[q] = jnp.where(r_i == sources[q], 1.0, 0.0).astype(BF16)
    for q in range(4):
        for plane in range(2):
            shf[q, :, plane * PL:(plane + 1) * PL] = jnp.dot(vs[plane], perm[q], preferred_element_type=F32)

    fetches[3].wait()

    @pl.loop(0, 18)
    def _(k):
        for plane in range(2):
            for j in range(3):
                row = jnp.broadcast_to(lk[j * 18 + k, plane:plane + 1, :], (8, PL))
                if j == 1:
                    low = pltpu.roll(row, LZ, 1)
                elif j == 2:
                    low = jnp.where(zz == 0, pltpu.roll(row, PL - LZ + 1, 1), pltpu.roll(row, 1, 1))
                for lt in range(2):
                    sl = slice(lt * 128, lt * 128 + 128)
                    bc[plane * 2 + lt, j * 18 + k] = row[:, sl]
                    if j > 0:
                        bc[plane * 2 + lt, 54 + j * 18 + k] = low[:, sl]
                    elif plane == 0:
                        bc[2 + lt, 54 + k] = row[:, sl]

    w_copy.wait()
    for plane in range(2):
        for r in range(24):
            w = jnp.broadcast_to(wloc[plane, r:r + 1, :] + wrem[plane, r:r + 1, :], (8, PL))
            for lt in range(2):
                bc[plane * 2 + lt, WROW + r] = w[:, lt * 128:lt * 128 + 128]

    def tile_work(i, dirs, load, store):
        half = i // 16
        t = lax.rem(i, 16) // 4
        quarter = lax.rem(i, 4)
        vg = half * 4 + quarter
        lanes = pl.ds(pl.multiple_of(t * 128, 128), 128)
        rows = pl.ds(pl.multiple_of(vg * 16, 16), 16)

        def field(j, back, f):
            if j == 0:
                ref = xm if back else xp
                return ref[f, rows, lanes].astype(F32).reshape(2, 8, 128)
            q = (j - 1) * 2 + back
            return shf[q, pl.ds(pl.multiple_of(f * NB + vg * 16, 16), 16), lanes].reshape(2, 8, 128)

        def coef(r):
            return bc[t, r][None]

        for c in range(3):
            acc = [[None, None] for _ in range(HEL)]
            if load:
                acc = [[part[i, (c * HEL + h) * 2 + ri] for ri in range(2)] for h in range(HEL)]
            for j in dirs:
                re = None
                im = None
                for c2 in range(3):
                    fr, fi = field(j, 0, c2), field(j, 0, 3 + c2)
                    gr, gi = field(j, 1, c2), field(j, 1, 3 + c2)
                    ur = coef(j * 18 + (c * 3 + c2) * 2)
                    ui = coef(j * 18 + (c * 3 + c2) * 2 + 1)
                    lr = coef(54 + j * 18 + (c2 * 3 + c) * 2)
                    li = coef(54 + j * 18 + (c2 * 3 + c) * 2 + 1)
                    a = ur * fr - ui * fi
                    b = ur * fi + ui * fr
                    a = a - lr * gr - li * gi
                    b = b - lr * gi + li * gr
                    re = a if re is None else re + a
                    im = b if im is None else im + b
                for h in range(HEL):
                    wr = coef(WROW + (h * 3 + j) * 2)
                    wi = coef(WROW + (h * 3 + j) * 2 + 1)
                    a = wr * re - wi * im
                    b = wr * im + wi * re
                    acc[h][0] = a if acc[h][0] is None else acc[h][0] + a
                    acc[h][1] = b if acc[h][1] is None else acc[h][1] + b
            if not store:
                for h in range(HEL):
                    for ri in range(2):
                        part[i, (c * HEL + h) * 2 + ri] = acc[h][ri]
                continue
            cols = pl.ds(pl.multiple_of(c * 2 * PL + t * 128, 128), 128)
            for h in range(HEL):
                for ri in range(2):
                    dst = pl.ds(pl.multiple_of(ri * NB + h % 2 * (NB // 2) + quarter * 16, 16), 16)
                    dbuf[half, h // 2, dst, cols] = acc[h][ri].reshape(16, 128).astype(BF16)

    def run_tiles(i0, i1, dirs=(0, 1, 2), load=False, store=True):
        @pl.loop(i0, i1)
        def _(i):
            tile_work(i, dirs, load, store)

    def send(k, part, n, rsem, where):
        ref = tbuf.at[k, part]
        g = remote(ref, ref, s_g.at[n], rsem, plane_dev(where))
        g.start()
        return g

    def to_sibling(k, n):
        ref = tbuf.at[k]
        remote(ref, ref, s_sib.at[n], r_sib.at[n], plane_dev(sib)).start()

    def along(k, n):
        ahead.append((send(k, ALL, 4 + 2 * n, r_g2.at[2 * n], right2),
                      send(k, ALL, 5 + 2 * n, r_g2.at[2 * n + 1], left2)))

    def over(k, n):
        ref = tbuf.at[k]
        g = remote(ref, ref, s_g.at[12 + n], r_g2.at[8 + n], dev(me, tm, 1 - op))
        g.start()
        across.append(g)
        to_sibling(k, n)

    def spread(k, n):
        along(k, n)
        over(k, n)

    run_tiles(0, 16, (1, 2), False, False)

    z_copy.wait()
    ahead = []
    across = []
    first = [send(came, ALL, 0, r_g1.at[0], right1), send(came, ALL, 1, r_g1.at[1], left1)]
    spread(came, 0)

    run_tiles(16, 24, (1, 2), False, False)
    run_tiles(24, 32, (1, 2), False, False)

    for cp in halo:
        cp.wait()

    @pl.loop(0, 18)
    def _(k):
        row = jnp.broadcast_to(halo_l[k, 1:2, :], (8, PL))
        for lt in range(2):
            bc[lt, 54 + k] = row[:, lt * 128:lt * 128 + 128]

    run_tiles(0, 8, (0,), True, True)

    for g in first:
        g.wait()
    kl, kr, ko = move1(came, 3), move1(came, 1), move1(came, 2)
    onward = [send(kl, LOW, 2, r_g1.at[2], right1), send(kr, HIGH, 3, r_g1.at[3], left1)]
    spread(kl, 1)
    spread(kr, 2)

    run_tiles(8, 16, (0,), True, True)

    def products(half):
        for hp in range(2):
            full = None
            for cp in range(6):
                prod = nt_dot(v[cp // 2, cp % 2].reshape(2 * NV, PL), dbuf[half, hp, :, cp * PL:(cp + 1) * PL])
                full = prod if full is None else full + prod
            re = full[:NV, :NB] + full[NV:, NB:]
            im = full[:NV, NB:] - full[NV:, :NB]
            pf[half, hp, :, :, 0:8] = re.reshape(NS // 2, 2, 8, NB)
            pf[half, hp, :, :, 8:16] = im.reshape(NS // 2, 2, 8, NB)
            pq[half, hp] = pf[half, hp, :, 1 - core].astype(BF16)
        g = remote(pq.at[half], ps.at[half], s_ps.at[half], r_ps.at[half], plane_dev(sib))
        g.start()
        return g

    def combine(half, g):
        g.wait()
        for hp in range(2):
            pbuf[hp, :, half] = (pf[half, hp, :, core] + ps[half, hp].astype(F32)).astype(BF16)

        @pl.loop(0, NS // 2)
        def _(d):
            owner = lax.rem(chip + d, NS // 2)
            remote(pbuf.at[1 - op, owner, half], rbuf.at[NS // 2 - 1 + d, half], s_rs, r_rs,
                   dev(owner * 2 + core, tm, 1 - op)).start()

        @pl.loop(1, NS // 2)
        def _(d):
            owner = lax.rem(chip + d, NS // 2)
            remote(pbuf.at[op, owner, half], rbuf.at[d - 1, half], s_rs, r_rs,
                   plane_dev(owner * 2 + core)).start()

    early = products(0)

    def turned(k, d):
        at = lax.rem(p2 + 2 * op, 4)
        return k + (lax.rem(at + d, 4) - at) * st2

    def settle(n):
        for g in ahead[n]:
            g.wait()
        across[n].wait()
        k = (came, kl, kr, ko)[n]
        to_sibling(turned(k, 3), n)
        to_sibling(turned(k, 1), n)
        to_sibling(turned(k, 2), n)

    settle(0)
    run_tiles(16, 20, (0,), True, True)
    combine(0, early)
    run_tiles(20, 24, (0,), True, True)

    for g in onward:
        g.wait()
    spread(ko, 3)

    run_tiles(24, 32, (0,), True, True)
    combine(1, products(1))

    for n in range(1, 4):
        settle(n)

    whole = remote(rbuf, rbuf, s_rs, r_rs, plane_dev(sib))
    whole.wait()

    def add(d, acc):
        return acc + rbuf[d].astype(F32)

    own = pf[:, op, chip, core] + ps[:, op, chip].astype(F32)
    obuf[op] = lax.fori_loop(0, NS // 2 - 1, add, own).astype(BF16)
    other = lax.fori_loop(NS // 2, NS - 1, add, rbuf[NS // 2 - 1].astype(F32))
    obuf[1 - op] = other.astype(BF16)

    for n in range(4):
        some = tbuf.at[pl.ds(0, 4)]
        remote(some, some, s_sib.at[n], r_sib.at[n], plane_dev(sib)).wait()

    lane = lax.broadcasted_iota(jnp.int32, (16, NB), 1)
    low = lane < NB // 2
    rows = [[], []]
    for o in range(2):
        a, b = obuf[o, 0].astype(F32), obuf[o, 1].astype(F32)
        rows[0].append(jnp.where(low, a, pltpu.roll(b, NB // 2, 1)))
        rows[1].append(jnp.where(low, pltpu.roll(a, NB // 2, 1), b))
    lines = []
    for h in range(2):
        ops = jnp.concatenate(rows[h], 1)
        o_r, o_i = ops[0:8], ops[8:16]
        lines.append(jnp.concatenate([o_r, -o_i], 1))
        lines.append(jnp.concatenate([o_i, o_r], 1))
    left = jnp.concatenate(lines, 0).astype(BF16)

    @pl.loop(0, 4)
    def _(q):
        for n in range(4):
            g = 4 * q + n
            right = jnp.concatenate([tbuf[2 * g], tbuf[2 * g + 1]], 1)
            res = jnp.dot(left, right, preferred_element_type=F32)
            out[:, g] = res.reshape(2, 2, 8, NV)


def shards(eigvecs, links, momenta, coef_num, coef_den, peram):
    v = jnp.transpose(eigvecs[0], (2, 3, 0, 1, 4))
    lk = links[0].reshape(54, 2, PL)
    me = lax.axis_index("space")
    core = me % 2
    row = 2 * lax.axis_index("op")
    cx, cy = me // 8, (me // 2) % 4
    row = 2 - row
    place = jnp.where(core == 0, cx * 4 + (cy + row) % 4, (cx + row) % 4 * 4 + cy)
    per = peram[0].reshape(NV, 16, 2, NV)
    piece = lax.dynamic_slice(per, (0, place, 0, core * 128), (NV, 1, 2, 128))
    piece = jnp.transpose(piece[:, 0], (1, 0, 2)).reshape(2 * NV, 128)
    hb = lambda x: pltpu.with_memory_space_constraint(x, pltpu.MemorySpace.HBM)
    vm = pl.BlockSpec(memory_space=pltpu.VMEM)
    hbm = pl.BlockSpec(memory_space=pltpu.MemorySpace.HBM)
    dma = pltpu.SemaphoreType.DMA
    out = pl.pallas_call(
        kernel,
        out_shape=jax.ShapeDtypeStruct((2, 16, 2, 8, NV), F32),
        in_specs=[hbm, hbm, hbm, hbm, vm, vm],
        out_specs=vm,
        scratch_shapes=[
            pltpu.SMEM((2, 3), jnp.int32),
            pltpu.SMEM((3, 2, HEL), jnp.int32),
            pltpu.SMEM((HEL,), jnp.int32),
            pltpu.VMEM((54, 2, PL), F32),
            dma((4,)),
            pltpu.VMEM((6, NB, 2 * PL), BF16),
            pltpu.VMEM((6, NB, 2 * PL), BF16),
            pltpu.VMEM((18, 2, PL), F32),
            pltpu.VMEM((2, 24, PL), F32),
            pltpu.VMEM((2, 24, PL), F32),
            pltpu.VMEM((4, 132, 8, 128), F32),
            pltpu.VMEM((2, 6 * NB, PL), BF16),
            pltpu.VMEM((4, PL, PL), BF16),
            pltpu.VMEM((4, 6 * NB, 2 * PL), F32),
            pltpu.VMEM((32, 24, 2, 8, 128), F32),
            pltpu.VMEM((2, 2, NV, 6 * PL), BF16),
            pltpu.VMEM((2, 2, NS // 2, 2, 16, NB), F32),
            pltpu.VMEM((2, 2, NS // 2, 16, NB), BF16),
            pltpu.VMEM((2, 2, NS // 2, 16, NB), BF16),
            pltpu.VMEM((2, NS // 2, 2, 16, NB), BF16),
            pltpu.VMEM((NS - 1, 2, 16, NB), BF16),
            pltpu.VMEM((NS, 2 * NV, 128), BF16),
            pltpu.VMEM((2, 2, 16, NB), BF16),
            dma((13,)), dma((6,)), dma((6,)), dma, dma, dma, dma, dma,
            dma((20,)), dma((4,)), dma((16,)), dma((4,)), dma((4,)), dma((2,)), dma((2,)), dma, dma,
        ],
        compiler_params=pltpu.CompilerParams(collective_id=0, has_side_effects=True,
                                             vmem_limit_bytes=48 * 1024 * 1024),
    )(hb(momenta), hb(jnp.transpose(coef_num, (2, 1, 0))), hb(coef_den), hb(lk), v, piece)
    return out.reshape(1, 2, 4, 4, 2, 8, NV)


def solution(mesh):
    return jax.shard_map(
        shards,
        mesh=mesh,
        in_specs=(
            P("tm", None, None, None, "space", None),
            P("tm", None, None, None, None, "space", None),
            P("op", None),
            P(None, "op", None),
            P(),
            P("tm", None, None, None, None, None),
        ),
        out_specs=P("tm", "op", None, None, None, "space", None),
        check_vma=False,
    )
```

```python
import functools
import math

import jax
import jax.numpy as jnp
from jax import lax
from jax.experimental import pallas as pl
from jax.experimental.pallas import tpu as pltpu
from jax.sharding import PartitionSpec as P

MESH = pl.DeviceIdType.MESH
F32 = jnp.float32
BF16 = jnp.bfloat16
NS = 32
NX = 64
LY = 32
LZ = 8
PL = LY * LZ
NV = 256
NB = NV // 2
HEL = 4
SCALE = 1.0 / math.sqrt(3.0 * NX * LY * LZ)
WROW = 108


def nt_dot(a, b):
    return lax.dot_general(a, b, (((1,), (1,)), ((), ())), preferred_element_type=F32)


def kernel(mom_h, num_h, den_h, lk_h, v, piece, out,
           mom, num, den, lk, s_in, xp, xm, halo_l, wloc, wrem, bc, vs, perm, shf, part, dbuf, pf, pq, ps, pbuf, rbuf, tbuf, obuf,
           s_halo, r_up, r_dn, r_lk, s_w, r_w, s_z, r_z, s_g, r_g1, r_g2, s_sib, r_sib, s_ps, r_ps, s_rs, r_rs):
    me = lax.axis_index("space")
    tm = lax.axis_index("tm")
    op = lax.axis_index("op")

    def dev(space, t, o):
        return {"space": space, "tm": t, "op": o}

    def plane_dev(space):
        return dev(space, tm, op)

    def remote(src, dst, ssem, rsem, where):
        return pltpu.make_async_remote_copy(src_ref=src, dst_ref=dst, send_sem=ssem, recv_sem=rsem,
                                            device_id=where, device_id_type=MESH)

    core = lax.rem(me, 2)
    chip = me // 2
    cx = chip // 4
    cy = lax.rem(chip, 4)
    sib = me + 1 - 2 * core
    nxt = lax.rem(me + 1, NS)
    prv = lax.rem(me + NS - 1, NS)

    st1 = 8 - 6 * core
    st2 = 2 + 6 * core
    p1 = cx * (1 - core) + cy * core
    p2 = cy * (1 - core) + cx * core
    LOW, HIGH, ALL = pl.ds(0, NV), pl.ds(NV, NV), pl.ds(0, 2 * NV)

    def move1(s, d):
        return s + (lax.rem(p1 + d, 4) - p1) * st1

    def move2(s, d):
        return s + (lax.rem(p2 + d, 4) - p2) * st2

    def held(s, o):
        return move2(s, 2 * o)

    right1, left1 = move1(me, 1), move1(me, 3)
    right2, left2 = move2(me, 1), move2(me, 3)

    fetches = [pltpu.make_async_copy(a, b, s_in.at[n])
               for n, (a, b) in enumerate(((mom_h, mom), (num_h, num), (den_h, den), (lk_h, lk)))]
    for cp in fetches:
        cp.start()

    barrier = pltpu.get_barrier_semaphore()

    def same_core(d):
        return lax.rem(chip + d, NS // 2) * 2 + core

    @pl.loop(1, NS // 2)
    def _(d):
        pl.semaphore_signal(barrier, inc=1, device_id=plane_dev(same_core(d)), device_id_type=MESH)

    @pl.loop(0, NS // 2)
    def _(d):
        pl.semaphore_signal(barrier, inc=1, device_id=dev(same_core(d), tm, 1 - op), device_id_type=MESH)

    cross = lax.rem(me + NS + 2 * core - 1, NS)
    for where in (plane_dev(cross), plane_dev(sib), dev(me, 1 - tm, 1 - op)):
        pl.semaphore_signal(barrier, inc=1, device_id=where, device_id_type=MESH)

    pl.semaphore_wait(barrier, NS + 2)

    z_copy = remote(piece, tbuf.at[held(me, 1 - op)], s_z, r_z, dev(me, 1 - tm, 1 - op))
    came = held(me, op)
    z_copy.start()

    brow = pl.ds(pl.multiple_of(op * NB, NB), NB)
    halo = []
    for f in range(6):
        ri, c = f // 3, f % 3
        up = remote(v.at[c, 0, ri, brow], xp.at[f, :, pl.ds(PL, PL)],
                    s_halo.at[f], r_up.at[f], plane_dev(prv))
        dn = remote(v.at[c, 1, ri, brow], xm.at[f, :, pl.ds(0, PL)],
                    s_halo.at[6 + f], r_dn.at[f], plane_dev(nxt))
        up.start()
        dn.start()
        halo += [up, dn]
    lk_copy = remote(lk_h.at[pl.ds(0, 18)], halo_l, s_halo.at[12], r_lk, plane_dev(nxt))
    lk_copy.start()
    halo.append(lk_copy)

    for cp in fetches[:3]:
        cp.wait()
    site = lax.broadcasted_iota(jnp.int32, (8, PL), 1)
    yy = site // LZ
    zz = site & (LZ - 1)
    inv = [SCALE / (jnp.zeros((8, PL), F32) + den[h].astype(F32)) for h in range(HEL)]
    for plane in range(2):
        phase = []
        for p in range(2):
            turn = (mom[p, 0] * (2 * me + plane)) & (NX - 1)
            turn = turn + 2 * ((mom[p, 1] * yy) & (LY - 1)) + 8 * ((mom[p, 2] * zz) & (LZ - 1))
            theta = (2.0 * math.pi / NX) * turn.astype(F32)
            phase.append((jnp.cos(theta), -jnp.sin(theta)))
        for h in range(HEL):
            for j in range(3):
                n0 = num[j, 0, h].astype(F32)
                n1 = num[j, 1, h].astype(F32)
                for ri in range(2):
                    w = (phase[0][ri] * n0 + phase[1][ri] * n1) * inv[h]
                    row = (h * 3 + j) * 2 + ri
                    wloc[plane, row:row + 1, :] = w[0:1]
    w_copy = remote(wloc, wrem, s_w, r_w, dev(me, tm, 1 - op))
    w_copy.start()

    for f in range(6):
        ri, c = f // 3, f % 3
        even = v[c, 0, ri, brow]
        odd = v[c, 1, ri, brow]
        xp[f, :, 0:PL] = odd
        xm[f, :, PL:2 * PL] = even
        vs[0, f * NB:(f + 1) * NB, :] = even
        vs[1, f * NB:(f + 1) * NB, :] = odd
    r_i = lax.broadcasted_iota(jnp.int32, (PL, PL), 0)
    c_i = lax.broadcasted_iota(jnp.int32, (PL, PL), 1)
    zc = c_i & (LZ - 1)
    sources = [(c_i + LZ) & (PL - 1), (c_i - LZ) & (PL - 1),
               c_i - zc + ((zc + 1) & (LZ - 1)), c_i - zc + ((zc - 1) & (LZ - 1))]
    for q in range(4):
        perm[q] = jnp.where(r_i == sources[q], 1.0, 0.0).astype(BF16)
    for q in range(4):
        for plane in range(2):
            shf[q, :, plane * PL:(plane + 1) * PL] = jnp.dot(vs[plane], perm[q], preferred_element_type=F32)

    fetches[3].wait()

    @pl.loop(0, 18)
    def _(k):
        for plane in range(2):
            for j in range(3):
                row = jnp.broadcast_to(lk[j * 18 + k, plane:plane + 1, :], (8, PL))
                if j == 1:
                    low = pltpu.roll(row, LZ, 1)
                elif j == 2:
                    low = jnp.where(zz == 0, pltpu.roll(row, PL - LZ + 1, 1), pltpu.roll(row, 1, 1))
                for lt in range(2):
                    sl = slice(lt * 128, lt * 128 + 128)
                    bc[plane * 2 + lt, j * 18 + k] = row[:, sl]
                    if j > 0:
                        bc[plane * 2 + lt, 54 + j * 18 + k] = low[:, sl]
                    elif plane == 0:
                        bc[2 + lt, 54 + k] = row[:, sl]

    w_copy.wait()
    for plane in range(2):
        for r in range(24):
            w = jnp.broadcast_to(wloc[plane, r:r + 1, :] + wrem[plane, r:r + 1, :], (8, PL))
            for lt in range(2):
                bc[plane * 2 + lt, WROW + r] = w[:, lt * 128:lt * 128 + 128]

    def tile_work(i, dirs, load, store):
        half = i // 16
        t = lax.rem(i, 16) // 4
        quarter = lax.rem(i, 4)
        vg = half * 4 + quarter
        lanes = pl.ds(pl.multiple_of(t * 128, 128), 128)
        rows = pl.ds(pl.multiple_of(vg * 16, 16), 16)

        def field(j, back, f):
            if j == 0:
                ref = xm if back else xp
                return ref[f, rows, lanes].astype(F32).reshape(2, 8, 128)
            q = (j - 1) * 2 + back
            return shf[q, pl.ds(pl.multiple_of(f * NB + vg * 16, 16), 16), lanes].reshape(2, 8, 128)

        def coef(r):
            return bc[t, r][None]

        for c in range(3):
            acc = [[None, None] for _ in range(HEL)]
            if load:
                acc = [[part[i, (c * HEL + h) * 2 + ri] for ri in range(2)] for h in range(HEL)]
            for j in dirs:
                re = None
                im = None
                for c2 in range(3):
                    fr, fi = field(j, 0, c2), field(j, 0, 3 + c2)
                    gr, gi = field(j, 1, c2), field(j, 1, 3 + c2)
                    ur = coef(j * 18 + (c * 3 + c2) * 2)
                    ui = coef(j * 18 + (c * 3 + c2) * 2 + 1)
                    lr = coef(54 + j * 18 + (c2 * 3 + c) * 2)
                    li = coef(54 + j * 18 + (c2 * 3 + c) * 2 + 1)
                    a = ur * fr - ui * fi
                    b = ur * fi + ui * fr
                    a = a - lr * gr - li * gi
                    b = b - lr * gi + li * gr
                    re = a if re is None else re + a
                    im = b if im is None else im + b
                for h in range(HEL):
                    wr = coef(WROW + (h * 3 + j) * 2)
                    wi = coef(WROW + (h * 3 + j) * 2 + 1)
                    a = wr * re - wi * im
                    b = wr * im + wi * re
                    acc[h][0] = a if acc[h][0] is None else acc[h][0] + a
                    acc[h][1] = b if acc[h][1] is None else acc[h][1] + b
            if not store:
                for h in range(HEL):
                    for ri in range(2):
                        part[i, (c * HEL + h) * 2 + ri] = acc[h][ri]
                continue
            cols = pl.ds(pl.multiple_of(c * 2 * PL + t * 128, 128), 128)
            for h in range(HEL):
                for ri in range(2):
                    dst = pl.ds(pl.multiple_of(ri * NB + h % 2 * (NB // 2) + quarter * 16, 16), 16)
                    dbuf[half, h // 2, dst, cols] = acc[h][ri].reshape(16, 128).astype(BF16)

    def run_tiles(i0, i1, dirs=(0, 1, 2), load=False, store=True):
        @pl.loop(i0, i1)
        def _(i):
            tile_work(i, dirs, load, store)

    def send(k, part, n, rsem, where):
        ref = tbuf.at[k, part]
        g = remote(ref, ref, s_g.at[n], rsem, plane_dev(where))
        g.start()
        return g

    def to_sibling(k, n):
        ref = tbuf.at[k]
        remote(ref, ref, s_sib.at[n], r_sib.at[n], plane_dev(sib)).start()

    def along(k, n):
        ahead.append((send(k, ALL, 4 + 2 * n, r_g2.at[2 * n], right2),
                      send(k, ALL, 5 + 2 * n, r_g2.at[2 * n + 1], left2)))

    def over(k, n):
        ref = tbuf.at[k]
        g = remote(ref, ref, s_g.at[12 + n], r_g2.at[8 + n], dev(me, tm, 1 - op))
        g.start()
        across.append(g)
        to_sibling(k, n)

    def spread(k, n):
        along(k, n)
        over(k, n)

    run_tiles(0, 16, (1, 2), False, False)

    z_copy.wait()
    ahead = []
    across = []
    first = [send(came, ALL, 0, r_g1.at[0], right1), send(came, ALL, 1, r_g1.at[1], left1)]
    spread(came, 0)

    run_tiles(16, 24, (1, 2), False, False)
    run_tiles(24, 32, (1, 2), False, False)

    for cp in halo:
        cp.wait()

    @pl.loop(0, 18)
    def _(k):
        row = jnp.broadcast_to(halo_l[k, 1:2, :], (8, PL))
        for lt in range(2):
            bc[lt, 54 + k] = row[:, lt * 128:lt * 128 + 128]

    run_tiles(0, 8, (0,), True, True)

    for g in first:
        g.wait()
    kl, kr, ko = move1(came, 3), move1(came, 1), move1(came, 2)
    onward = [send(kl, LOW, 2, r_g1.at[2], right1), send(kr, HIGH, 3, r_g1.at[3], left1)]
    spread(kl, 1)
    spread(kr, 2)

    run_tiles(8, 16, (0,), True, True)

    def products(half):
        for hp in range(2):
            full = None
            for cp in range(6):
                prod = nt_dot(v[cp // 2, cp % 2].reshape(2 * NV, PL), dbuf[half, hp, :, cp * PL:(cp + 1) * PL])
                full = prod if full is None else full + prod
            re = full[:NV, :NB] + full[NV:, NB:]
            im = full[:NV, NB:] - full[NV:, :NB]
            pf[half, hp, :, :, 0:8] = re.reshape(NS // 2, 2, 8, NB)
            pf[half, hp, :, :, 8:16] = im.reshape(NS // 2, 2, 8, NB)
            pq[half, hp] = pf[half, hp, :, 1 - core].astype(BF16)
        g = remote(pq.at[half], ps.at[half], s_ps.at[half], r_ps.at[half], plane_dev(sib))
        g.start()
        return g

    def combine(half, g):
        g.wait()
        for hp in range(2):
            pbuf[hp, :, half] = (pf[half, hp, :, core] + ps[half, hp].astype(F32)).astype(BF16)

        @pl.loop(0, NS // 2)
        def _(d):
            owner = lax.rem(chip + d, NS // 2)
            remote(pbuf.at[1 - op, owner, half], rbuf.at[NS // 2 - 1 + d, half], s_rs, r_rs,
                   dev(owner * 2 + core, tm, 1 - op)).start()

        @pl.loop(1, NS // 2)
        def _(d):
            owner = lax.rem(chip + d, NS // 2)
            remote(pbuf.at[op, owner, half], rbuf.at[d - 1, half], s_rs, r_rs,
                   plane_dev(owner * 2 + core)).start()

    early = products(0)

    def turned(k, d):
        at = lax.rem(p2 + 2 * op, 4)
        return k + (lax.rem(at + d, 4) - at) * st2

    def settle(n):
        for g in ahead[n]:
            g.wait()
        across[n].wait()
        k = (came, kl, kr, ko)[n]
        to_sibling(turned(k, 3), n)
        to_sibling(turned(k, 1), n)
        to_sibling(turned(k, 2), n)

    settle(0)
    run_tiles(16, 20, (0,), True, True)
    combine(0, early)
    run_tiles(20, 24, (0,), True, True)

    for g in onward:
        g.wait()
    spread(ko, 3)

    run_tiles(24, 32, (0,), True, True)
    combine(1, products(1))

    for n in range(1, 4):
        settle(n)

    whole = remote(rbuf, rbuf, s_rs, r_rs, plane_dev(sib))
    whole.wait()

    def add(d, acc):
        return acc + rbuf[d].astype(F32)

    own = pf[:, op, chip, core] + ps[:, op, chip].astype(F32)
    obuf[op] = lax.fori_loop(0, NS // 2 - 1, add, own).astype(BF16)
    other = lax.fori_loop(NS // 2, NS - 1, add, rbuf[NS // 2 - 1].astype(F32))
    obuf[1 - op] = other.astype(BF16)

    for n in range(4):
        some = tbuf.at[pl.ds(0, 4)]
        remote(some, some, s_sib.at[n], r_sib.at[n], plane_dev(sib)).wait()

    lane = lax.broadcasted_iota(jnp.int32, (16, NB), 1)
    low = lane < NB // 2
    rows = [[], []]
    for o in range(2):
        a, b = obuf[o, 0].astype(F32), obuf[o, 1].astype(F32)
        rows[0].append(jnp.where(low, a, pltpu.roll(b, NB // 2, 1)))
        rows[1].append(jnp.where(low, pltpu.roll(a, NB // 2, 1), b))
    lines = []
    for h in range(2):
        ops = jnp.concatenate(rows[h], 1)
        o_r, o_i = ops[0:8], ops[8:16]
        lines.append(jnp.concatenate([o_r, -o_i], 1))
        lines.append(jnp.concatenate([o_i, o_r], 1))
    left = jnp.concatenate(lines, 0).astype(BF16)

    @pl.loop(0, 4)
    def _(q):
        for n in range(4):
            g = 4 * q + n
            right = jnp.concatenate([tbuf[2 * g], tbuf[2 * g + 1]], 1)
            res = jnp.dot(left, right, preferred_element_type=F32)
            out[:, g] = res.reshape(2, 2, 8, NV)


def shards(eigvecs, links, momenta, coef_num, coef_den, peram):
    v = jnp.transpose(eigvecs[0], (2, 3, 0, 1, 4))
    lk = links[0].reshape(54, 2, PL)
    me = lax.axis_index("space")
    core = me % 2
    row = 2 * lax.axis_index("op")
    cx, cy = me // 8, (me // 2) % 4
    row = 2 - row
    place = jnp.where(core == 0, cx * 4 + (cy + row) % 4, (cx + row) % 4 * 4 + cy)
    per = peram[0].reshape(NV, 16, 2, NV)
    piece = lax.dynamic_slice(per, (0, place, 0, core * 128), (NV, 1, 2, 128))
    piece = jnp.transpose(piece[:, 0], (1, 0, 2)).reshape(2 * NV, 128)
    hb = lambda x: pltpu.with_memory_space_constraint(x, pltpu.MemorySpace.HBM)
    vm = pl.BlockSpec(memory_space=pltpu.VMEM)
    hbm = pl.BlockSpec(memory_space=pltpu.MemorySpace.HBM)
    dma = pltpu.SemaphoreType.DMA
    out = pl.pallas_call(
        kernel,
        out_shape=jax.ShapeDtypeStruct((2, 16, 2, 8, NV), F32),
        in_specs=[hbm, hbm, hbm, hbm, vm, vm],
        out_specs=vm,
        scratch_shapes=[
            pltpu.SMEM((2, 3), jnp.int32),
            pltpu.SMEM((3, 2, HEL), jnp.int32),
            pltpu.SMEM((HEL,), jnp.int32),
            pltpu.VMEM((54, 2, PL), F32),
            dma((4,)),
            pltpu.VMEM((6, NB, 2 * PL), BF16),
            pltpu.VMEM((6, NB, 2 * PL), BF16),
            pltpu.VMEM((18, 2, PL), F32),
            pltpu.VMEM((2, 24, PL), F32),
            pltpu.VMEM((2, 24, PL), F32),
            pltpu.VMEM((4, 132, 8, 128), F32),
            pltpu.VMEM((2, 6 * NB, PL), BF16),
            pltpu.VMEM((4, PL, PL), BF16),
            pltpu.VMEM((4, 6 * NB, 2 * PL), F32),
            pltpu.VMEM((32, 24, 2, 8, 128), F32),
            pltpu.VMEM((2, 2, NV, 6 * PL), BF16),
            pltpu.VMEM((2, 2, NS // 2, 2, 16, NB), F32),
            pltpu.VMEM((2, 2, NS // 2, 16, NB), BF16),
            pltpu.VMEM((2, 2, NS // 2, 16, NB), BF16),
            pltpu.VMEM((2, NS // 2, 2, 16, NB), BF16),
            pltpu.VMEM((NS - 1, 2, 16, NB), BF16),
            pltpu.VMEM((NS, 2 * NV, 128), BF16),
            pltpu.VMEM((2, 2, 16, NB), BF16),
            dma((13,)), dma((6,)), dma((6,)), dma, dma, dma, dma, dma,
            dma((20,)), dma((4,)), dma((16,)), dma((4,)), dma((4,)), dma((2,)), dma((2,)), dma, dma,
        ],
        compiler_params=pltpu.CompilerParams(collective_id=0, has_side_effects=True,
                                             vmem_limit_bytes=48 * 1024 * 1024),
    )(hb(momenta), hb(jnp.transpose(coef_num, (2, 1, 0))), hb(coef_den), hb(lk), v, piece)
    return out.reshape(1, 2, 4, 4, 2, 8, NV)


def solution(mesh):
    return jax.shard_map(
        shards,
        mesh=mesh,
        in_specs=(
            P("tm", None, None, None, "space", None),
            P("tm", None, None, None, None, "space", None),
            P("op", None),
            P(None, "op", None),
            P(),
            P("tm", None, None, None, None, None),
        ),
        out_specs=P("tm", "op", None, None, None, "space", None),
        check_vma=False,
    )
```
